32 devices in a mesh: section: 4 (over y, x), ctx: 8 (over z, core).
Axes of the slice: x: 2, y: 2, z: 4, core: 2. Of those that a mesh axis runs over, the one named last changes fastest.
Arguments:
- fwd_in: bfloat16 [4, 1152, 1024], P('section', 'ctx'), may hold values from -6 to 6
- bwd_saved: bfloat16 [4, 1152, 1024], P('section', 'ctx'), may hold values from -6 to 6
- bwd_cot: bfloat16 [4, 1152, 1024], P('section', 'ctx'), may hold values from -6 to 6
- new_tokens: bfloat16 [1024, 1024], P('ctx'), may hold values from -6 to 6
- loss_cot: bfloat16 [1024, 1024], P('ctx'), may hold values from -6 to 6
- gain: bfloat16 [4, 1024], P('section'), may hold values from 0.099609375 to 1.8984375
- w_query: bfloat16 [4, 1024, 1024], P('section'), may hold values from -2 to 2
- w_keyval: bfloat16 [4, 1024, 512], P('section'), may hold values from -2 to 2
- w_out: bfloat16 [4, 1024, 1024], P('section'), may hold values from -0.1875 to 0.1875
Outputs:
- fwd_next: bfloat16 [4, 1152, 1024], P('section', 'ctx')
- cot_next: bfloat16 [4, 1152, 1024], P('section', 'ctx')
The draws below stay inside these ranges and needn't reach their ends.
All inputs are finite; a program needn't handle non-finite values.
Results may differ from the reference program's by a relative error of at most 0.012.
The reference program's roundings to bfloat16 on the way count: a program that leaves them out, or rounds other values in their place, can miss the bound.
Values may be sent and summed in bfloat16 or wider, within the bound.
A program may use at most 64 MiB of HBM per device.

```python
import jax
import jax.numpy as jnp
from jax import lax

D = 1024
HEADS = 16
KV_HEADS = 4
HEAD_DIM = 64
GROUP = 8
MEM_DEV = 16
SEG_DEV = 128
ROWS_DEV = 144
SEG = 1024
LAYERS = 4
SEGMENTS = 1
ROWS = 1152
N_CTX = 8


def weight_base(key, salt, shape):
    values = jax.random.normal(jax.random.fold_in(key, salt), shape, jnp.float32)
    return jnp.clip(values, -6.0, 6.0) * D ** (-0.5)


def draw_w_query(key, part):
    values = weight_base(key, 7201, (LAYERS, D, HEADS * HEAD_DIM))
    return jnp.clip(values, -2.0, 2.0).astype(jnp.bfloat16)


def draw_w_keyval(key, part):
    values = weight_base(key, 7202, (LAYERS, D, 2 * KV_HEADS * HEAD_DIM))
    return jnp.clip(values, -2.0, 2.0).astype(jnp.bfloat16)


def drawn_rows(key, salt):
    noise = jax.random.normal(jax.random.fold_in(key, salt), (LAYERS, ROWS, D), jnp.float32)
    return jnp.clip(noise, -6.0, 6.0)


def draw_fwd_in(key, part):
    return drawn_rows(key, 7301).astype(jnp.bfloat16)


def draw_bwd_saved(key, part):
    return drawn_rows(key, 7302).astype(jnp.bfloat16)


def block_scale(key, extent, pieces, low, high):
    factor_of = 1.0
    for axis_at, shards_of in pieces:
        heights = jax.random.uniform(jax.random.fold_in(jax.random.fold_in(key, 6), axis_at), (shards_of,), jnp.float32, low / len(pieces), high / len(pieces))
        factor_of = factor_of * jnp.repeat(jnp.exp(heights), extent[axis_at] // shards_of).reshape((-1,) + (1,) * (len(extent) - 1 - axis_at))
    return factor_of


def normal_values(rng, dims, deviation, bound, split=(), kind=jnp.bfloat16):
    entries = jax.random.normal(rng, dims, jnp.float32) * deviation
    if len(split) > 0:
        entries = block_scale(rng, dims, split, -0.22, 0.18) * entries
    return jnp.clip(entries, min=-bound, max=bound).astype(kind)


def setup_inputs(seed: int = 0) -> dict:
    key_list = jax.random.split(jax.random.key(seed), 10)
    fwd_in = draw_fwd_in(jax.random.fold_in(key_list[9], 71), 0)
    bwd_saved = draw_bwd_saved(jax.random.fold_in(key_list[9], 71), 0)
    bwd_cot = normal_values(key_list[2], (LAYERS, ROWS, D), 1.0, 6.0, ((0, 4), (1, 8)))
    new_tokens = normal_values(key_list[3], (SEGMENTS * SEG, D), 1.0, 6.0, ((0, 8),))
    loss_cot = normal_values(key_list[4], (SEGMENTS * SEG, D), 1.0, 6.0, ((0, 8),))
    gain = jnp.clip(1.0 + 0.18 * jax.random.normal(key_list[5], (LAYERS, D), jnp.float32), 0.099609375, 1.8984375).astype(jnp.bfloat16)
    w_query = draw_w_query(jax.random.fold_in(key_list[9], 71), 0)
    w_keyval = draw_w_keyval(jax.random.fold_in(key_list[9], 71), 0)
    w_out = normal_values(key_list[8], (LAYERS, HEADS * HEAD_DIM, D), (HEADS * HEAD_DIM) ** -0.5, 0.1875, ((0, 4),))
    return dict(fwd_in=fwd_in, bwd_saved=bwd_saved, bwd_cot=bwd_cot, new_tokens=new_tokens, loss_cot=loss_cot, gain=gain, w_query=w_query, w_keyval=w_keyval, w_out=w_out)


epsilon = 1e-05

def segment_allowed():
    rows = jnp.arange(GROUP * ROWS_DEV, dtype=jnp.int32)
    block = rows // ROWS_DEV
    inner = rows % ROWS_DEV
    is_memory = inner < MEM_DEV
    position = block * SEG_DEV + inner - MEM_DEV
    return is_memory[None, :] | is_memory[:, None] | (position[None, :] <= position[:, None])

def normalize(hidden):
    values = hidden.astype(jnp.float32)
    scale = lax.rsqrt(lax.optimization_barrier(jnp.mean(values * values, axis=-1, keepdims=True)) + epsilon)
    return (values, scale)

def split_heads(query, keyval):
    rows_q = query.shape[0]
    rows_k = keyval.shape[0]
    shared = HEADS // KV_HEADS
    width = KV_HEADS * HEAD_DIM
    grouped = query.reshape(rows_q, KV_HEADS, shared, HEAD_DIM).transpose(1, 2, 0, 3)
    keys = keyval[:, :width].reshape(rows_k, KV_HEADS, HEAD_DIM).transpose(1, 0, 2)
    values = keyval[:, width:].reshape(rows_k, KV_HEADS, HEAD_DIM).transpose(1, 0, 2)
    return (grouped, keys, values)

def head_probs(q_head, k_head, allowed):
    scores = jnp.einsum('grd,kd->grk', q_head.astype(jnp.float32), k_head.astype(jnp.float32), precision=lax.Precision.HIGHEST) * HEAD_DIM ** (-0.5)
    scores = jnp.where(allowed[None], scores, -1e+30)
    top = lax.optimization_barrier(jnp.max(scores, axis=-1, keepdims=True))
    expd = jnp.exp(scores - top)
    return expd / lax.optimization_barrier(jnp.sum(expd, axis=-1, keepdims=True))

def attend_forward(query, keyval, allowed):
    grouped, keys, values = split_heads(query, keyval)

    def one_head(items):
        q_head, k_head, v_head = items
        weights = head_probs(q_head, k_head, allowed).astype(jnp.bfloat16)
        return jnp.einsum('grk,kd->grd', weights.astype(jnp.float32), v_head.astype(jnp.float32), precision=lax.Precision.HIGHEST)
    outs = lax.map(one_head, (grouped, keys, values))
    return outs.transpose(2, 0, 1, 3).reshape(query.shape[0], HEADS * HEAD_DIM).astype(jnp.bfloat16)

def attend_backward(query, keyval, allowed, grad_mixed):
    grouped, keys, values = split_heads(query, keyval)
    shared = HEADS // KV_HEADS
    grads = grad_mixed.reshape(query.shape[0], KV_HEADS, shared, HEAD_DIM).transpose(1, 2, 0, 3)

    def one_head(items):
        q_head, k_head, v_head, g_head = items
        probs = head_probs(q_head, k_head, allowed)
        weights = probs.astype(jnp.bfloat16)
        dprobs = jnp.einsum('grd,kd->grk', g_head.astype(jnp.float32), v_head.astype(jnp.float32), precision=lax.Precision.HIGHEST)
        delta = lax.optimization_barrier(jnp.sum(dprobs * probs, axis=-1, keepdims=True))
        dscores = (probs * (dprobs - delta) * HEAD_DIM ** (-0.5)).astype(jnp.bfloat16)
        grad_q = jnp.einsum('grk,kd->grd', dscores.astype(jnp.float32), k_head.astype(jnp.float32), precision=lax.Precision.HIGHEST)
        grad_k = jnp.einsum('grk,grd->kd', dscores.astype(jnp.float32), q_head.astype(jnp.float32), precision=lax.Precision.HIGHEST)
        grad_v = jnp.einsum('grk,grd->kd', weights.astype(jnp.float32), g_head.astype(jnp.float32), precision=lax.Precision.HIGHEST)
        return (grad_q, grad_k, grad_v)
    grad_q, grad_k, grad_v = lax.map(one_head, (grouped, keys, values, grads))
    rows_k = keyval.shape[0]
    grad_query = grad_q.transpose(2, 0, 1, 3).reshape(query.shape[0], HEADS * HEAD_DIM).astype(jnp.bfloat16)
    grad_keys = grad_k.transpose(1, 0, 2).reshape(rows_k, KV_HEADS * HEAD_DIM)
    grad_values = grad_v.transpose(1, 0, 2).reshape(rows_k, KV_HEADS * HEAD_DIM)
    return (grad_query, jnp.concatenate([grad_keys, grad_values], axis=1))

def project(hidden, gain_row, w_query, w_keyval):
    values, scale = normalize(hidden)
    normed = (values * scale * gain_row.astype(jnp.float32)).astype(jnp.bfloat16)
    query = jnp.dot(normed, w_query, preferred_element_type=jnp.float32).astype(jnp.bfloat16)
    keyval = jnp.dot(normed, w_keyval, preferred_element_type=jnp.float32).astype(jnp.bfloat16)
    return (values, scale, query, keyval)

def layer_forward(hidden, gain_row, w_query, w_keyval, w_out, allowed):
    values, scale, query, keyval = project(hidden, gain_row, w_query, w_keyval)
    mixed = attend_forward(query, keyval, allowed)
    return (values + jnp.dot(mixed, w_out, preferred_element_type=jnp.float32)).astype(jnp.bfloat16)

def layer_backward(hidden, grad_out, gain_row, w_query, w_keyval, w_out, allowed):
    values, scale, query, keyval = project(hidden, gain_row, w_query, w_keyval)
    grad_mixed = jnp.dot(grad_out, w_out.T, preferred_element_type=jnp.float32).astype(jnp.bfloat16)
    grad_query, grad_kv = attend_backward(query, keyval, allowed, grad_mixed)
    grad_keyval = grad_kv.astype(jnp.bfloat16)
    grad_normed = jnp.dot(grad_query, w_query.T, preferred_element_type=jnp.float32)
    grad_normed = grad_normed + jnp.dot(grad_keyval, w_keyval.T, preferred_element_type=jnp.float32)
    plain = values * scale
    pushed = gain_row.astype(jnp.float32) * grad_normed
    grad_in = grad_out.astype(jnp.float32) + scale * (pushed - plain * lax.optimization_barrier(jnp.mean(pushed * plain, axis=-1, keepdims=True)))
    return grad_in.astype(jnp.bfloat16)

def reference(fwd_in, bwd_saved, bwd_cot, new_tokens, loss_cot, gain, w_query, w_keyval, w_out):
    allowed = segment_allowed()
    rows_seg = GROUP * ROWS_DEV

    def forward_layer(items):
        hidden, gain_row, wq_layer, wkv_layer, wo_layer = items
        segs = hidden.reshape(SEGMENTS, rows_seg, D)
        outs = lax.map(lambda seg: layer_forward(seg, gain_row, wq_layer, wkv_layer, wo_layer, allowed), segs)
        return outs.reshape(ROWS, D)

    def backward_layer(items):
        hidden, grad_out, gain_row, wq_layer, wkv_layer, wo_layer = items
        segs = hidden.reshape(SEGMENTS, rows_seg, D)
        grad_segs = grad_out.reshape(SEGMENTS, rows_seg, D)
        outs = lax.map(lambda pair: layer_backward(pair[0], pair[1], gain_row, wq_layer, wkv_layer, wo_layer, allowed), (segs, grad_segs))
        return outs.reshape(ROWS, D)
    outs = lax.map(forward_layer, (fwd_in, gain, w_query, w_keyval, w_out))
    grads = lax.map(backward_layer, (bwd_saved, bwd_cot, gain, w_query, w_keyval, w_out))
    last_blocks = outs[LAYERS - 1].reshape(N_CTX, ROWS_DEV, D)
    first = jnp.concatenate([last_blocks[:, :MEM_DEV], new_tokens.reshape(N_CTX, SEG_DEV, D)], axis=1)
    fwd_next = jnp.concatenate([first.reshape(1, ROWS, D), outs[:-1]], axis=0)
    first_grads = grads[0].reshape(N_CTX, ROWS_DEV, D)
    last = jnp.concatenate([first_grads[:, :MEM_DEV], loss_cot.reshape(N_CTX, SEG_DEV, D)], axis=1)
    cot_next = jnp.concatenate([grads[1:], last.reshape(1, ROWS, D)], axis=0)
    return (fwd_next, cot_next)
```

```python
import functools

import jax
import jax.numpy as jnp
from jax import lax
from jax.experimental import pallas as pl
from jax.experimental.pallas import tpu as pltpu
from jax.sharding import PartitionSpec as P

HEADS = 16
KV_HEADS = 4
HEAD_DIM = 64
GROUP = 8
PAIR = 2
CHIPS = GROUP // PAIR
LOCAL = KV_HEADS // PAIR
SHARED = HEADS // KV_HEADS
LANES = 128
PIECES = 4
UNROLL = 3

epsilon = 1e-05
far = 1 << 30

bf16 = jnp.bfloat16
f32 = jnp.float32
NT = (((1,), (1,)), ((), ()))
NN = (((1,), (0,)), ((), ()))


def mul(a, b, dims=NN):
    return lax.dot_general(a, b, dims, preferred_element_type=f32)


def kernel(
    sections, mem,
    xf_h, xb_h, cot_h, gain_h, wq_h, wkv_h, wo_h,
    outf_h, outb_h,
    xf, xb, cot, gain_v, wq, wkv, wo, normed, kvf, kvb, kvt, qf, qb, gb, kpos,
    sd, ex, cat, acc, gsend, grecv, gpass, gsum, kvown, qx_send, qx_recv,
    gq_my, gq_send, gq_recv, mix_my, mix_send, mix_recv, of, ob,
    local_sem, pair_send, pair_recv, kv_send, kv_recv, gr_send, gr_recv, sec_send, sec_recv,
    hop_send, hop_recv,
):
    rows = xf_h.shape[0]
    width = xf_h.shape[1]
    both = PAIR * rows
    total = GROUP * rows
    half = width // PAIR
    tokens = rows - mem
    slab = LANES // (PAIR * SHARED)
    rounds = rows // slab // UNROLL
    early = rounds - 1
    cut = early * UNROLL * slab

    ctx = lax.axis_index("ctx")
    section = lax.axis_index("section")
    member = lax.rem(ctx, GROUP)
    base = ctx - member
    core = lax.rem(member, PAIR)
    chip = member // PAIR
    other = 1 - core
    partner = base + chip * PAIR + other

    after = lax.rem(section + 1, sections)
    before = lax.rem(section + sections - 1, sections)
    barrier = pltpu.get_barrier_semaphore()
    for k in range(1, GROUP):
        pl.semaphore_signal(
            barrier, inc=1, device_id={"ctx": base + lax.rem(member + k, GROUP)},
            device_id_type=pl.DeviceIdType.MESH,
        )
    for neighbour in (after, before):
        pl.semaphore_signal(
            barrier, inc=1, device_id={"section": neighbour},
            device_id_type=pl.DeviceIdType.MESH,
        )

    loads = []
    for at, (src, dst) in enumerate(
        [
            (xb_h, xb), (gain_h, gain_v), (wkv_h, wkv), (wq_h, wq), (xf_h, xf),
            (cot_h, cot), (wo_h, wo),
        ]
    ):
        copy = pltpu.make_async_copy(src, dst, local_sem.at[at])
        copy.start()
        loads.append(copy)
    load_xb, load_gain, load_wkv, load_wq, load_xf, load_cot, load_wo = loads

    def remote(src, dst, send, recv, where):
        return pltpu.make_async_remote_copy(
            src_ref=src, dst_ref=dst, send_sem=send, recv_sem=recv,
            device_id=where, device_id_type=pl.DeviceIdType.MESH,
        )

    pair_copies = []

    def pair_copy(at, src, dst):
        copy = remote(src, dst, pair_send.at[at], pair_recv.at[at], {"ctx": partner})
        copy.start()
        pair_copies.append(copy)

    def pair_arrived(at, dst):
        remote(dst, dst, pair_send.at[at], pair_recv.at[at], {"ctx": partner}).wait_recv()

    for b in range(GROUP):
        inner = lax.broadcasted_iota(jnp.int32, (rows, LANES), 0)
        kpos[b * rows : (b + 1) * rows, :] = jnp.where(
            inner < mem, -1, b * tokens + inner - mem
        )

    def norm(x):
        values = x.astype(f32)
        scale = lax.rsqrt(jnp.mean(values * values, axis=-1, keepdims=True) + epsilon)
        return values, scale

    def make_normed(x_ref):
        values, scale = norm(x_ref[...])
        normed[...] = (values * scale * gain_v[...].astype(f32)).astype(bf16)

    last = CHIPS - 1
    is_end = jnp.logical_or(chip == 0, chip == last)
    is_middle = jnp.logical_not(is_end)
    opposite = last - chip
    adjacent = jnp.where(chip == 0, 1, last - 1)
    hop_from = jnp.where(chip == 1, last, 0)
    hop_to = last - hop_from
    sum_via = jnp.where(chip == 0, 1, last - 1)
    sum_from = jnp.where(chip == 1, 0, last)

    def peer(k):
        return lax.rem(member + k, GROUP)

    def source(k):
        return lax.rem(member + GROUP - k, GROUP)

    def is_far(one):
        return jnp.logical_and(is_end, one // PAIR == opposite)

    order = sorted(range(1, GROUP), key=lambda k: abs(k - GROUP // 2))

    def project_kv(kv_ref, kind):
        keyval = mul(normed[...], wkv[...])
        for h in range(KV_HEADS):
            at = h * HEAD_DIM
            after_keys = KV_HEADS * HEAD_DIM + at
            kvown[kind, h] = jnp.concatenate(
                [keyval[:, at : at + HEAD_DIM], keyval[:, after_keys : after_keys + HEAD_DIM]],
                axis=1,
            ).astype(bf16)
        for g in range(LOCAL):
            kv_ref[g, pl.ds(member * rows, rows), :] = kvown[kind, core * LOCAL + g]

    def kv_copy(kv_ref, kind, g, k):
        to = peer(k)
        return remote(
            kvown.at[kind, lax.rem(to, PAIR) * LOCAL + g],
            kv_ref.at[g, pl.ds(member * rows, rows)],
            kv_send.at[kind, g, k], kv_recv.at[kind, g, k], {"ctx": base + to},
        )

    def send_kv(kv_ref, kind, g):
        for k in order:
            @pl.when(jnp.logical_not(is_far(peer(k))))
            def _():
                kv_copy(kv_ref, kind, g, k).start()

    def finish_kv(kv_ref, kind):
        for g in range(LOCAL):
            for k in order:
                @pl.when(jnp.logical_not(is_far(peer(k))))
                def _():
                    kv_copy(kv_ref, kind, g, k).wait_send()

            @pl.when(is_middle)
            def _():
                hop_copy(kv_ref, kind, g).wait_send()

    def hop_copy(kv_ref, kind, g):
        place = kv_ref.at[g, pl.ds(hop_from * both, both)]
        return remote(
            place, place, hop_send.at[kind, g], hop_recv.at[kind, g],
            {"ctx": base + hop_to * PAIR + core},
        )

    def kv_wait(kv_ref, kind, g, one):
        k = lax.rem(member + GROUP - one, GROUP)
        place = kv_ref.at[g, pl.ds(one * rows, rows)]
        remote(
            place, place, kv_send.at[kind, g, k], kv_recv.at[kind, g, k], {"ctx": base + one}
        ).wait_recv()

    def hop_kv(kv_ref, kind, g):
        @pl.when(is_middle)
        def _():
            for c in range(PAIR):
                kv_wait(kv_ref, kind, g, hop_from * PAIR + c)
            hop_copy(kv_ref, kind, g).start()

    def near_kv(kv_ref, kind, g):
        @pl.when(is_end)
        def _():
            for c in range(PAIR):
                kv_wait(kv_ref, kind, g, adjacent * PAIR + c)

    def kv_arrived(kv_ref, kind, g, near_done=False):
        for k in range(1, GROUP):
            one = source(k)
            done = jnp.logical_and(is_middle, one // PAIR == hop_from)
            if near_done:
                done = jnp.logical_or(done, jnp.logical_and(is_end, one // PAIR == adjacent))

            @pl.when(jnp.logical_not(jnp.logical_or(is_far(one), done)))
            def _():
                kv_wait(kv_ref, kind, g, one)

        @pl.when(is_end)
        def _():
            place = kv_ref.at[g, pl.ds(opposite * both, both)]
            remote(
                place, place, hop_send.at[kind, g], hop_recv.at[kind, g],
                {"ctx": base + opposite * PAIR + core},
            ).wait_recv()

    def gr_copy(g, k):
        to = peer(k)
        return remote(
            gsend.at[g, pl.ds(to * rows, rows)], grecv.at[k, g],
            gr_send.at[g, k], gr_recv.at[g, k], {"ctx": base + to},
        )

    def is_summed(one):
        return jnp.logical_and(is_middle, one // PAIR == last - sum_from)

    def sum_copy(g, where):
        return remote(
            gsend.at[g, pl.ds(opposite * both, both)], gpass.at[g],
            hop_send.at[2, g], hop_recv.at[2, g], {"ctx": base + where * PAIR + core},
        )

    def send_sums(g):
        gsend[g] = acc[g].astype(bf16)

        @pl.when(is_end)
        def _():
            sum_copy(g, sum_via).start()

        for k in order:
            to = peer(k)

            @pl.when(jnp.logical_not(jnp.logical_or(is_far(to), is_summed(to))))
            def _():
                gr_copy(g, k).start()

    def hop_sums(g):
        @pl.when(is_middle)
        def _():
            sum_copy(g, sum_from).wait_recv()
            place = pl.ds((last - sum_from) * both, both)
            gsend[g, place, :] = (acc[g, place, :] + gpass[g].astype(f32)).astype(bf16)
            for k in order:
                @pl.when(is_summed(peer(k)))
                def _():
                    gr_copy(g, k).start()

    def finish_sums(g):
        @pl.when(is_end)
        def _():
            sum_copy(g, sum_via).wait_send()

        for k in order:
            @pl.when(jnp.logical_not(is_far(peer(k))))
            def _():
                gr_copy(g, k).wait_send()

    def spread(matrix, dst, block, upper, factor):
        rounded = matrix.astype(f32) * factor
        zero = jnp.zeros((rows, HEAD_DIM), f32)
        for g in range(LOCAL):
            for h in range(SHARED):
                at = (g * SHARED + h) * HEAD_DIM
                piece = rounded[:, at : at + HEAD_DIM]
                parts = [zero, piece] if upper else [piece, zero]
                wide = jnp.concatenate(parts, axis=1).astype(bf16)
                for i in range(rows // slab):
                    to = i * LANES + (block * SHARED + h) * slab
                    dst[g, to : to + slab, :] = wide[i * slab : (i + 1) * slab, :]

    scale_by = HEAD_DIM ** (-0.5)
    my_cols = pl.ds(pl.multiple_of(core * half, half), half)
    their_cols = pl.ds(pl.multiple_of(other * half, half), half)

    def make_query(at, q_ref):
        qx_send[at] = mul(normed[...], wq[:, their_cols]).astype(bf16)
        spread(mul(normed[...], wq[:, my_cols]).astype(bf16), q_ref, 0, False, scale_by)

    load_xb.wait()
    load_gain.wait()
    make_normed(xb)
    load_wkv.wait()
    project_kv(kvb, 0)
    load_wq.wait()
    make_query(0, qb)
    load_xf.wait()
    make_normed(xf)
    project_kv(kvf, 1)
    pl.semaphore_wait(barrier, GROUP + 1)
    send_kv(kvb, 0, 0)
    pair_copy(0, qx_send.at[0], qx_recv.at[0])
    load_cot.wait()
    load_wo.wait()
    qx_send[2] = mul(cot[...], wo[their_cols, :], NT).astype(bf16)
    pair_copy(2, qx_send.at[2], qx_recv.at[2])
    spread(mul(cot[...], wo[my_cols, :], NT).astype(bf16), gb, 0, True, 1.0)
    make_query(1, qf)
    pair_copy(1, qx_send.at[1], qx_recv.at[1])
    pair_arrived(0, qx_recv.at[0])
    spread(qx_recv[0], qb, 1, False, scale_by)
    pair_arrived(2, qx_recv.at[2])
    spread(qx_recv[2], gb, 1, True, 1.0)
    near_kv(kvb, 0, 0)
    hop_kv(kvb, 0, 0)
    send_kv(kvb, 0, 1)
    pair_arrived(1, qx_recv.at[1])
    spread(qx_recv[1], qf, 1, False, scale_by)

    step = total // PIECES

    def query_positions(i):
        lane = lax.broadcasted_iota(jnp.int32, (1, LANES), 1)
        block = jnp.where(lane < LANES // PAIR, member, chip * PAIR + other)
        inner = i * slab + lax.rem(lane, slab)
        return jnp.where(inner < mem, far, block * tokens + inner - mem)

    parts = [slice(p * step, (p + 1) * step) for p in range(PIECES)]

    def put_heads(g, i, turned, mine_ref, theirs_ref):
        place = pl.ds(pl.multiple_of(i * slab, slab), slab)
        for block, ref in enumerate((mine_ref, theirs_ref)):
            for h in range(0, SHARED, 2):
                at = (block * SHARED + h) * slab
                pair = jnp.concatenate(
                    [turned[at : at + slab, :], turned[at + slab : at + 2 * slab, :]], axis=1
                )
                to = (g * SHARED + h) * HEAD_DIM
                ref[place, to : to + LANES] = pair.astype(bf16)

    def backward_chunk(g, chunks):
        starts = [pl.multiple_of(i * LANES, LANES) for i in chunks]
        pairs = [
            jnp.concatenate([qb[g, pl.ds(at, LANES), :], gb[g, pl.ds(at, LANES), :]], axis=0)
            for at in starts
        ]
        for u, i in enumerate(chunks):
            position = query_positions(i)
            top = None
            for part in parts:
                product = mul(kvb[g, part, :], pairs[u], NT)
                scores = jnp.where(kpos[part, :] <= position, product[:, :LANES], -1e30)
                sd[u, part, :LANES] = scores
                sd[u, part, LANES:] = product[:, LANES:]
                peak = jnp.max(scores, axis=0, keepdims=True)
                top = peak if top is None else jnp.maximum(top, peak)
            norm_sum = jnp.zeros((1, LANES), f32)
            delta = jnp.zeros((1, LANES), f32)
            for part in parts:
                expd = jnp.exp(sd[u, part, :LANES] - top)
                ex[u, part, :] = expd
                norm_sum += jnp.sum(expd, axis=0, keepdims=True)
                delta += jnp.sum(expd * sd[u, part, LANES:], axis=0, keepdims=True)
            inverse = 1.0 / norm_sum
            delta = delta * inverse
            at = u * 2 * LANES
            for part in parts:
                probs = ex[u, part, :] * inverse
                cat[part, at + LANES : at + 2 * LANES] = probs.astype(bf16)
                cat[part, at : at + LANES] = (probs * (sd[u, part, LANES:] - delta)).astype(bf16)
        everything = jnp.concatenate(pairs, axis=0)
        for part in parts:
            acc[g, part, :] += mul(cat[part, :], everything)
        for u, i in enumerate(chunks):
            at = u * 2 * LANES
            turned = mul(kvt[:HEAD_DIM, :], cat[:, at : at + LANES])
            put_heads(g, i, turned.T * scale_by, gq_my, gq_send)

    def forward_chunk(g, chunks):
        for u, i in enumerate(chunks):
            start = pl.multiple_of(i * LANES, LANES)
            queries = qf[g, pl.ds(start, LANES), :]
            position = query_positions(i)
            top = None
            for part in parts:
                product = mul(kvf[g, part, :], queries, NT)
                scores = jnp.where(kpos[part, :] <= position, product, -1e30)
                sd[u, part, :LANES] = scores
                peak = jnp.max(scores, axis=0, keepdims=True)
                top = peak if top is None else jnp.maximum(top, peak)
            norm_sum = jnp.zeros((1, LANES), f32)
            for part in parts:
                expd = jnp.exp(sd[u, part, :LANES] - top)
                ex[u, part, :] = expd
                norm_sum += jnp.sum(expd, axis=0, keepdims=True)
            inverse = 1.0 / norm_sum
            for part in parts:
                cat[part, u * LANES : (u + 1) * LANES] = (ex[u, part, :] * inverse).astype(bf16)
        turned = mul(kvt[HEAD_DIM:, :], cat[:, : len(chunks) * LANES])
        for u, i in enumerate(chunks):
            put_heads(g, i, turned[:, u * LANES : (u + 1) * LANES].T, mix_my, mix_send)

    def run(chunk, g, begin, end, actions):
        def body(i, carry):
            for at, action in actions.items():
                pl.when(i == at)(action)
            chunk(g, [i * UNROLL + u for u in range(UNROLL)])
            return carry

        lax.fori_loop(begin, end, body, 0)

    def turn(kv_ref, g):
        kvt[...] = kv_ref[g].astype(f32).T.astype(bf16)

    def after_first():
        hop_kv(kvb, 0, 1)
        send_kv(kvf, 1, 0)

    def after_sums():
        hop_kv(kvf, 1, 0)
        send_kv(kvf, 1, 1)

    backward_actions = [
        {1: after_first},
        {0: after_sums, 1: lambda: hop_sums(0), 2: lambda: hop_kv(kvf, 1, 1)},
    ]
    for g in range(LOCAL):
        kv_arrived(kvb, 0, g, g == 0)
        turn(kvb, g)
        acc[g] = jnp.zeros((total, LANES), f32)
        run(backward_chunk, g, 0, rounds, backward_actions[g])
        send_sums(g)
    pair_copy(3, gq_send, gq_recv)

    def shift(at, src, dst, where, begin, end, edge, arrive_edge):
        def copy(index, first, stop):
            place = pl.ds(first, stop - first)
            return remote(
                src.at[place], dst.at[place],
                sec_send.at[at, index], sec_recv.at[at, index], {"section": where},
            )

        small = copy(0, begin, mem) if begin < mem else None
        large = copy(1, max(begin, mem), end)
        if small is not None:
            small.start()

        @pl.when(section != edge)
        def _():
            large.start()

        def finish():
            if small is not None:
                small.wait()

            @pl.when(section != edge)
            def _():
                large.wait_send()

            @pl.when(section != arrive_edge)
            def _():
                large.wait_recv()

        return finish

    def project_out(at, begin, end):
        place = slice(begin, end)
        pair_copy(4 + at, mix_send.at[place], mix_recv.at[place])
        made = xf[place, :].astype(f32) + mul(mix_my[place, :], wo[my_cols, :])
        pair_arrived(4 + at, mix_recv.at[place])
        made += mul(mix_recv[place, :], wo[their_cols, :])
        of[place, :] = made.astype(bf16)
        return shift(at, of, outf_h, after, begin, end, sections - 1, 0)

    for g in range(LOCAL):
        if g == 1:
            hop_sums(1)
        kv_arrived(kvf, 1, g)
        turn(kvf, g)
        run(forward_chunk, g, 0, early, {})
    finish_early = project_out(0, 0, cut)

    for g in range(LOCAL):
        own = acc[g, pl.ds(member * rows, rows), :]
        cross = None
        for k in range(1, GROUP):
            one = source(k)

            @pl.when(is_far(one))
            def _():
                grecv[k, g] = jnp.zeros((rows, LANES), bf16)

            @pl.when(jnp.logical_not(is_far(one)))
            def _():
                place = grecv.at[k, g]
                remote(
                    place, place, gr_send.at[g, k], gr_recv.at[g, k], {"ctx": base + one}
                ).wait_recv()

            value = grecv[k, g].astype(f32)
            if k % PAIR == 0:
                own = own + value
            else:
                cross = value if cross is None else cross + value
        gsum[core * LOCAL + g] = own
        gsum[other * LOCAL + g] = cross
    pair_arrived(3, gq_recv)
    columns = [gsum[h, :, :HEAD_DIM] for h in range(KV_HEADS)]
    columns += [gsum[h, :, HEAD_DIM:] for h in range(KV_HEADS)]
    grad_kv = jnp.concatenate(columns, axis=1).astype(bf16)
    grad_normed = mul(grad_kv, wkv[...], NT)
    grad_normed += mul(gq_my[...], wq[:, my_cols], NT)
    grad_normed += mul(gq_recv[...], wq[:, their_cols], NT)
    values, scale = norm(xb[...])
    plain = values * scale
    pushed = gain_v[...].astype(f32) * grad_normed
    grad_in = cot[...].astype(f32) + scale * (
        pushed - plain * jnp.mean(pushed * plain, axis=-1, keepdims=True)
    )
    ob[...] = grad_in.astype(bf16)
    finish_b = shift(2, ob, outb_h, before, 0, rows, 0, sections - 1)

    for g in range(LOCAL):
        turn(kvf, g)
        run(forward_chunk, g, early, rounds, {})
    finish_late = project_out(1, cut, rows)

    for copy in pair_copies:
        copy.wait_send()
    finish_kv(kvb, 0)
    finish_kv(kvf, 1)
    for g in range(LOCAL):
        finish_sums(g)
    finish_early()
    finish_late()
    finish_b()


def shards(fwd_in, bwd_saved, bwd_cot, new_tokens, loss_cot, gain, w_query, w_keyval, w_out):
    section_now = lax.axis_index("section")
    sections = lax.axis_size("section")
    rows, width = fwd_in.shape[1:]
    mem = rows - new_tokens.shape[0]
    both = PAIR * rows
    total = GROUP * rows
    stack = SHARED * both
    half = width // PAIR
    anywhere = pl.BlockSpec(memory_space=pl.ANY)
    far_memory = pl.BlockSpec(memory_space=pltpu.HBM)
    block = jax.ShapeDtypeStruct((rows, width), bf16)
    vmem = pltpu.VMEM
    dma = pltpu.SemaphoreType.DMA
    arrived, returned = pl.pallas_call(
        functools.partial(kernel, sections, mem),
        out_shape=(block, block),
        in_specs=[far_memory] * 7,
        out_specs=(anywhere, anywhere),
        scratch_shapes=[
            vmem((rows, width), bf16), vmem((rows, width), bf16), vmem((rows, width), bf16),
            vmem((1, width), bf16),
            vmem(w_query.shape[1:], bf16), vmem(w_keyval.shape[1:], bf16), vmem(w_out.shape[1:], bf16),
            vmem((rows, width), bf16),
            vmem((LOCAL, total, LANES), bf16), vmem((LOCAL, total, LANES), bf16),
            vmem((LANES, total), bf16),
            vmem((LOCAL, stack, LANES), bf16), vmem((LOCAL, stack, LANES), bf16),
            vmem((LOCAL, stack, LANES), bf16),
            vmem((total, LANES), jnp.int32),
            vmem((UNROLL, total, 2 * LANES), f32), vmem((UNROLL, total, LANES), f32),
            vmem((total, UNROLL * 2 * LANES), bf16),
            vmem((LOCAL, total, LANES), f32), vmem((LOCAL, total, LANES), bf16),
            vmem((GROUP, LOCAL, rows, LANES), bf16), vmem((LOCAL, both, LANES), bf16),
            vmem((KV_HEADS, rows, LANES), f32), vmem((2, KV_HEADS, rows, LANES), bf16),
            vmem((3, rows, half), bf16), vmem((3, rows, half), bf16),
            vmem((rows, half), bf16), vmem((rows, half), bf16), vmem((rows, half), bf16),
            vmem((rows, half), bf16), vmem((rows, half), bf16), vmem((rows, half), bf16),
            vmem((rows, width), bf16), vmem((rows, width), bf16),
            dma((7,)), dma((6,)), dma((6,)),
            dma((2, LOCAL, GROUP)), dma((2, LOCAL, GROUP)),
            dma((LOCAL, GROUP)), dma((LOCAL, GROUP)),
            dma((3, 2)), dma((3, 2)),
            dma((3, LOCAL)), dma((3, LOCAL)),
        ],
        compiler_params=pltpu.CompilerParams(
            collective_id=0, has_side_effects=True, vmem_limit_bytes=60500 * 1024
        ),
    )(fwd_in[0], bwd_saved[0], bwd_cot[0], gain, w_query[0], w_keyval[0], w_out[0])
    token_row = lax.broadcasted_iota(jnp.int32, (rows, 1), 0) >= mem
    edge = jnp.pad(new_tokens, ((mem, 0), (0, 0)))
    fwd_next = jnp.where(token_row & (section_now == 0), edge, arrived)[None]
    edge = jnp.pad(loss_cot, ((mem, 0), (0, 0)))
    cot_next = jnp.where(token_row & (section_now == sections - 1), edge, returned)[None]
    return (fwd_next, cot_next)


def solution(mesh):
    return jax.shard_map(
        shards,
        mesh=mesh,
        in_specs=(
            P("section", "ctx", None),
            P("section", "ctx", None),
            P("section", "ctx", None),
            P("ctx", None),
            P("ctx", None),
            P("section", None),
            P("section", None, None),
            P("section", None, None),
            P("section", None, None),
        ),
        out_specs=(P("section", "ctx", None), P("section", "ctx", None)),
        check_vma=False,
    )
```

```python
import functools

import jax
import jax.numpy as jnp
from jax import lax
from jax.experimental import pallas as pl
from jax.experimental.pallas import tpu as pltpu
from jax.sharding import PartitionSpec as P

HEADS = 16
KV_HEADS = 4
HEAD_DIM = 64
GROUP = 8
PAIR = 2
CHIPS = GROUP // PAIR
LOCAL = KV_HEADS // PAIR
SHARED = HEADS // KV_HEADS
LANES = 128
PIECES = 4
UNROLL = 3

epsilon = 1e-05
far = 1 << 30

bf16 = jnp.bfloat16
f32 = jnp.float32
NT = (((1,), (1,)), ((), ()))
NN = (((1,), (0,)), ((), ()))


def mul(a, b, dims=NN):
    return lax.dot_general(a, b, dims, preferred_element_type=f32)


def kernel(
    sections, mem,
    xf_h, xb_h, cot_h, gain_h, wq_h, wkv_h, wo_h,
    outf_h, outb_h,
    xf, xb, cot, gain_v, wq, wkv, wo, normed, kvf, kvb, kvt, qf, qb, gb, kpos,
    sd, ex, cat, acc, gsend, grecv, gpass, gsum, kvown, qx_send, qx_recv,
    gq_my, gq_send, gq_recv, mix_my, mix_send, mix_recv, of, ob,
    local_sem, pair_send, pair_recv, kv_send, kv_recv, gr_send, gr_recv, sec_send, sec_recv,
    hop_send, hop_recv,
):
    rows = xf_h.shape[0]
    width = xf_h.shape[1]
    both = PAIR * rows
    total = GROUP * rows
    half = width // PAIR
    tokens = rows - mem
    slab = LANES // (PAIR * SHARED)
    rounds = rows // slab // UNROLL

    ctx = lax.axis_index("ctx")
    section = lax.axis_index("section")
    member = lax.rem(ctx, GROUP)
    base = ctx - member
    core = lax.rem(member, PAIR)
    chip = member // PAIR
    other = 1 - core
    partner = base + chip * PAIR + other

    after = lax.rem(section + 1, sections)
    before = lax.rem(section + sections - 1, sections)
    barrier = pltpu.get_barrier_semaphore()
    for k in range(1, GROUP):
        pl.semaphore_signal(
            barrier, inc=1, device_id={"ctx": base + lax.rem(member + k, GROUP)},
            device_id_type=pl.DeviceIdType.MESH,
        )
    for neighbour in (after, before):
        pl.semaphore_signal(
            barrier, inc=1, device_id={"section": neighbour},
            device_id_type=pl.DeviceIdType.MESH,
        )

    loads = []
    for at, (src, dst) in enumerate(
        [
            (xb_h, xb), (gain_h, gain_v), (wkv_h, wkv), (wq_h, wq), (xf_h, xf),
            (cot_h, cot), (wo_h, wo),
        ]
    ):
        copy = pltpu.make_async_copy(src, dst, local_sem.at[at])
        copy.start()
        loads.append(copy)
    load_xb, load_gain, load_wkv, load_wq, load_xf, load_cot, load_wo = loads

    def remote(src, dst, send, recv, where):
        return pltpu.make_async_remote_copy(
            src_ref=src, dst_ref=dst, send_sem=send, recv_sem=recv,
            device_id=where, device_id_type=pl.DeviceIdType.MESH,
        )

    pair_copies = []

    def pair_copy(at, src, dst):
        copy = remote(src, dst, pair_send.at[at], pair_recv.at[at], {"ctx": partner})
        copy.start()
        pair_copies.append(copy)

    def pair_arrived(at, dst):
        remote(dst, dst, pair_send.at[at], pair_recv.at[at], {"ctx": partner}).wait_recv()

    for b in range(GROUP):
        inner = lax.broadcasted_iota(jnp.int32, (rows, LANES), 0)
        kpos[b * rows : (b + 1) * rows, :] = jnp.where(
            inner < mem, -1, b * tokens + inner - mem
        )

    def norm(x):
        values = x.astype(f32)
        scale = lax.rsqrt(jnp.mean(values * values, axis=-1, keepdims=True) + epsilon)
        return values, scale

    def make_normed(x_ref):
        values, scale = norm(x_ref[...])
        normed[...] = (values * scale * gain_v[...].astype(f32)).astype(bf16)

    last = CHIPS - 1
    is_end = jnp.logical_or(chip == 0, chip == last)
    is_middle = jnp.logical_not(is_end)
    opposite = last - chip
    nearest_end = jnp.where(chip == 1, 0, last)
    adjacent = jnp.where(is_end, jnp.where(chip == 0, 1, last - 1), nearest_end)
    hop_at = jnp.where(chip == 0, last - 1, 1)
    hop_from = jnp.where(chip == 1, last, 0)
    hop_to = last - hop_from
    sum_via = jnp.where(chip == 0, 1, last - 1)
    sum_from = jnp.where(chip == 1, 0, last)

    def peer(k):
        return lax.rem(member + k, GROUP)

    def source(k):
        return lax.rem(member + GROUP - k, GROUP)

    def is_far(one):
        return jnp.logical_and(is_end, one // PAIR == opposite)

    order = sorted(range(1, GROUP), key=lambda k: abs(k - GROUP // 2))

    def project_kv(kv_ref, kind):
        keyval = mul(normed[...], wkv[...])
        for h in range(KV_HEADS):
            at = h * HEAD_DIM
            after_keys = KV_HEADS * HEAD_DIM + at
            kvown[kind, h] = jnp.concatenate(
                [keyval[:, at : at + HEAD_DIM], keyval[:, after_keys : after_keys + HEAD_DIM]],
                axis=1,
            ).astype(bf16)
        for g in range(LOCAL):
            kv_ref[g, pl.ds(member * rows, rows), :] = kvown[kind, core * LOCAL + g]

    def kv_copy(kv_ref, kind, g, k):
        to = peer(k)
        return remote(
            kvown.at[kind, lax.rem(to, PAIR) * LOCAL + g],
            kv_ref.at[g, pl.ds(member * rows, rows)],
            kv_send.at[kind, g, k], kv_recv.at[kind, g, k], {"ctx": base + to},
        )

    def is_first(one):
        away = one // PAIR
        ends = jnp.logical_and(is_end, jnp.logical_or(away == hop_at, away == chip))
        return jnp.logical_or(ends, jnp.logical_and(is_middle, away == adjacent))

    def send_kv(kv_ref, kind, g, phase=None):
        for k in order:
            use = jnp.logical_not(is_far(peer(k)))
            if phase is not None:
                first = is_first(peer(k))
                use = jnp.logical_and(use, first if phase == 0 else jnp.logical_not(first))

            @pl.when(use)
            def _():
                kv_copy(kv_ref, kind, g, k).start()

    def finish_kv(kv_ref, kind):
        for g in range(LOCAL):
            for k in order:
                @pl.when(jnp.logical_not(is_far(peer(k))))
                def _():
                    kv_copy(kv_ref, kind, g, k).wait_send()

            @pl.when(is_middle)
            def _():
                hop_copy(kv_ref, kind, g).wait_send()

    def hop_copy(kv_ref, kind, g):
        place = kv_ref.at[g, pl.ds(hop_from * both, both)]
        return remote(
            place, place, hop_send.at[kind, g], hop_recv.at[kind, g],
            {"ctx": base + hop_to * PAIR + core},
        )

    def kv_wait(kv_ref, kind, g, one):
        k = lax.rem(member + GROUP - one, GROUP)
        place = kv_ref.at[g, pl.ds(one * rows, rows)]
        remote(
            place, place, kv_send.at[kind, g, k], kv_recv.at[kind, g, k], {"ctx": base + one}
        ).wait_recv()

    def hop_kv(kv_ref, kind, g):
        @pl.when(is_middle)
        def _():
            for c in range(PAIR):
                kv_wait(kv_ref, kind, g, hop_from * PAIR + c)
            hop_copy(kv_ref, kind, g).start()

    def near_kv(kv_ref, kind, g):
        @pl.when(is_end)
        def _():
            for c in range(PAIR):
                kv_wait(kv_ref, kind, g, adjacent * PAIR + c)

    def kv_arrived(kv_ref, kind, g, near_done=False):
        for k in range(1, GROUP):
            one = source(k)
            done = jnp.logical_and(is_middle, one // PAIR == hop_from)
            if near_done:
                done = jnp.logical_or(done, jnp.logical_and(is_end, one // PAIR == adjacent))

            @pl.when(jnp.logical_not(jnp.logical_or(is_far(one), done)))
            def _():
                kv_wait(kv_ref, kind, g, one)

        @pl.when(is_end)
        def _():
            place = kv_ref.at[g, pl.ds(opposite * both, both)]
            remote(
                place, place, hop_send.at[kind, g], hop_recv.at[kind, g],
                {"ctx": base + opposite * PAIR + core},
            ).wait_recv()

    def gr_copy(g, k):
        to = peer(k)
        return remote(
            gsend.at[g, pl.ds(to * rows, rows)], grecv.at[k, g],
            gr_send.at[g, k], gr_recv.at[g, k], {"ctx": base + to},
        )

    def is_summed(one):
        return jnp.logical_and(is_middle, one // PAIR == last - sum_from)

    def sum_copy(g, where):
        return remote(
            gsend.at[g, pl.ds(opposite * both, both)], gpass.at[g],
            hop_send.at[2, g], hop_recv.at[2, g], {"ctx": base + where * PAIR + core},
        )

    def send_sums(g):
        gsend[g] = acc[g].astype(bf16)

        @pl.when(is_end)
        def _():
            sum_copy(g, sum_via).start()

        for k in order:
            to = peer(k)

            @pl.when(jnp.logical_not(jnp.logical_or(is_far(to), is_summed(to))))
            def _():
                gr_copy(g, k).start()

    def hop_sums(g):
        @pl.when(is_middle)
        def _():
            sum_copy(g, sum_from).wait_recv()
            place = pl.ds((last - sum_from) * both, both)
            gsend[g, place, :] = (acc[g, place, :] + gpass[g].astype(f32)).astype(bf16)
            for k in order:
                @pl.when(is_summed(peer(k)))
                def _():
                    gr_copy(g, k).start()

    def finish_sums(g):
        @pl.when(is_end)
        def _():
            sum_copy(g, sum_via).wait_send()

        for k in order:
            @pl.when(jnp.logical_not(is_far(peer(k))))
            def _():
                gr_copy(g, k).wait_send()

    def spread(matrix, dst, block, upper, factor):
        rounded = matrix.astype(f32) * factor
        zero = jnp.zeros((rows, HEAD_DIM), f32)
        for g in range(LOCAL):
            for h in range(SHARED):
                at = (g * SHARED + h) * HEAD_DIM
                piece = rounded[:, at : at + HEAD_DIM]
                parts = [zero, piece] if upper else [piece, zero]
                wide = jnp.concatenate(parts, axis=1).astype(bf16)
                for i in range(rows // slab):
                    to = i * LANES + (block * SHARED + h) * slab
                    dst[g, to : to + slab, :] = wide[i * slab : (i + 1) * slab, :]

    scale_by = HEAD_DIM ** (-0.5)
    my_cols = pl.ds(pl.multiple_of(core * half, half), half)
    their_cols = pl.ds(pl.multiple_of(other * half, half), half)

    def make_query(at, q_ref):
        qx_send[at] = mul(normed[...], wq[:, their_cols]).astype(bf16)
        spread(mul(normed[...], wq[:, my_cols]).astype(bf16), q_ref, 0, False, scale_by)

    load_xb.wait()
    load_gain.wait()
    make_normed(xb)
    load_wkv.wait()
    project_kv(kvb, 0)
    pl.semaphore_wait(barrier, GROUP + 1)
    send_kv(kvb, 0, 0, 0)
    load_wq.wait()
    make_query(0, qb)
    send_kv(kvb, 0, 0, 1)
    pair_copy(0, qx_send.at[0], qx_recv.at[0])
    load_cot.wait()
    load_wo.wait()
    qx_send[2] = mul(cot[...], wo[their_cols, :], NT).astype(bf16)
    pair_copy(2, qx_send.at[2], qx_recv.at[2])
    spread(mul(cot[...], wo[my_cols, :], NT).astype(bf16), gb, 0, True, 1.0)
    load_xf.wait()
    make_normed(xf)
    project_kv(kvf, 1)
    pair_arrived(0, qx_recv.at[0])
    spread(qx_recv[0], qb, 1, False, scale_by)
    pair_arrived(2, qx_recv.at[2])
    spread(qx_recv[2], gb, 1, True, 1.0)
    near_kv(kvb, 0, 0)
    hop_kv(kvb, 0, 0)
    send_kv(kvb, 0, 1)
    make_query(1, qf)
    pair_copy(1, qx_send.at[1], qx_recv.at[1])

    step = total // PIECES

    def query_positions(i):
        lane = lax.broadcasted_iota(jnp.int32, (1, LANES), 1)
        block = jnp.where(lane < LANES // PAIR, member, chip * PAIR + other)
        inner = i * slab + lax.rem(lane, slab)
        return jnp.where(inner < mem, far, block * tokens + inner - mem)

    parts = [slice(p * step, (p + 1) * step) for p in range(PIECES)]

    def put_heads(g, i, turned, mine_ref, theirs_ref):
        place = pl.ds(pl.multiple_of(i * slab, slab), slab)
        for block, ref in enumerate((mine_ref, theirs_ref)):
            for h in range(0, SHARED, 2):
                at = (block * SHARED + h) * slab
                pair = jnp.concatenate(
                    [turned[at : at + slab, :], turned[at + slab : at + 2 * slab, :]], axis=1
                )
                to = pl.multiple_of((g * SHARED + h) * HEAD_DIM, LANES)
                ref[place, pl.ds(to, LANES)] = pair.astype(bf16)

    def backward_chunk(g, chunks):
        starts = [pl.multiple_of(i * LANES, LANES) for i in chunks]
        pairs = [
            jnp.concatenate([qb[g, pl.ds(at, LANES), :], gb[g, pl.ds(at, LANES), :]], axis=0)
            for at in starts
        ]
        for u, i in enumerate(chunks):
            position = query_positions(i)
            top = None
            for part in parts:
                product = mul(kvb[g, part, :], pairs[u], NT)
                scores = jnp.where(kpos[part, :] <= position, product[:, :LANES], -1e30)
                sd[u, part, :LANES] = scores
                sd[u, part, LANES:] = product[:, LANES:]
                peak = jnp.max(scores, axis=0, keepdims=True)
                top = peak if top is None else jnp.maximum(top, peak)
            norm_sum = jnp.zeros((1, LANES), f32)
            delta = jnp.zeros((1, LANES), f32)
            for part in parts:
                expd = jnp.exp(sd[u, part, :LANES] - top)
                ex[u, part, :] = expd
                norm_sum += jnp.sum(expd, axis=0, keepdims=True)
                delta += jnp.sum(expd * sd[u, part, LANES:], axis=0, keepdims=True)
            inverse = 1.0 / norm_sum
            delta = delta * inverse
            at = u * 2 * LANES
            for part in parts:
                probs = ex[u, part, :] * inverse
                cat[part, at + LANES : at + 2 * LANES] = probs.astype(bf16)
                cat[part, at : at + LANES] = (probs * (sd[u, part, LANES:] - delta)).astype(bf16)
        everything = jnp.concatenate(pairs, axis=0)
        for part in parts:
            acc[g, part, :] += mul(cat[part, :], everything)
        for u, i in enumerate(chunks):
            at = u * 2 * LANES
            turned = mul(kvt[g], cat[:, at : at + LANES])
            put_heads(g, i, turned.T * scale_by, gq_my, gq_send)

    def forward_chunk(g, chunks):
        for u, i in enumerate(chunks):
            start = pl.multiple_of(i * LANES, LANES)
            queries = qf[g, pl.ds(start, LANES), :]
            position = query_positions(i)
            top = None
            for part in parts:
                product = mul(kvf[g, part, :], queries, NT)
                scores = jnp.where(kpos[part, :] <= position, product, -1e30)
                sd[u, part, :LANES] = scores
                peak = jnp.max(scores, axis=0, keepdims=True)
                top = peak if top is None else jnp.maximum(top, peak)
            norm_sum = jnp.zeros((1, LANES), f32)
            for part in parts:
                expd = jnp.exp(sd[u, part, :LANES] - top)
                ex[u, part, :] = expd
                norm_sum += jnp.sum(expd, axis=0, keepdims=True)
            inverse = 1.0 / norm_sum
            for part in parts:
                cat[part, u * LANES : (u + 1) * LANES] = (ex[u, part, :] * inverse).astype(bf16)
        turned = mul(kvt[g], cat[:, : len(chunks) * LANES])
        for u, i in enumerate(chunks):
            put_heads(g, i, turned[:, u * LANES : (u + 1) * LANES].T, mix_my, mix_send)

    def run(chunk, g, begin, end, actions):
        def body(i, carry):
            for at, action in actions.items():
                pl.when(i == at)(action)
            chunk(g, [i * UNROLL + u for u in range(UNROLL)])
            return carry

        lax.fori_loop(begin, end, body, 0)

    def turn(kv_ref, g, first):
        whole = kv_ref[g].astype(f32).T
        kvt[g] = whole[first : first + HEAD_DIM, :].astype(bf16)

    def after_first():
        hop_kv(kvf, 1, 0)
        send_kv(kvf, 1, 1)

    backward_actions = [
        {0: lambda: send_kv(kvf, 1, 0), 1: lambda: hop_kv(kvb, 0, 1), 2: after_first},
        {1: lambda: hop_kv(kvf, 1, 1), 2: lambda: hop_sums(0)},
    ]
    for g in range(LOCAL):
        kv_arrived(kvb, 0, g, g == 0)
        turn(kvb, g, 0)
        acc[g] = jnp.zeros((total, LANES), f32)
        run(backward_chunk, g, 0, rounds, backward_actions[g])
        send_sums(g)
    pair_copy(3, gq_send, gq_recv)
    pair_arrived(1, qx_recv.at[1])
    spread(qx_recv[1], qf, 1, False, scale_by)

    def shift(at, src, dst, where, begin, end, edge, arrive_edge):
        def copy(index, first, stop):
            place = pl.ds(first, stop - first)
            return remote(
                src.at[place], dst.at[place],
                sec_send.at[at, index], sec_recv.at[at, index], {"section": where},
            )

        small = copy(0, begin, mem) if begin < mem else None
        large = copy(1, max(begin, mem), end)
        if small is not None:
            small.start()

        @pl.when(section != edge)
        def _():
            large.start()

        def finish():
            if small is not None:
                small.wait()

            @pl.when(section != edge)
            def _():
                large.wait_send()

            @pl.when(section != arrive_edge)
            def _():
                large.wait_recv()

        return finish

    def forward_part(at):
        begin, end = at * UNROLL * slab, (at + 1) * UNROLL * slab

        def body(g, carry):
            forward_chunk(g, [at * UNROLL + u for u in range(UNROLL)])
            return carry

        lax.fori_loop(0, LOCAL, body, 0)
        place = slice(begin, end)
        pair_copy(4 + at, mix_send.at[place], mix_recv.at[place])
        made = xf[place, :].astype(f32) + mul(mix_my[place, :], wo[my_cols, :])
        pair_arrived(4 + at, mix_recv.at[place])
        made += mul(mix_recv[place, :], wo[their_cols, :])
        of[place, :] = made.astype(bf16)
        return shift(at, of, outf_h, after, begin, end, sections - 1, 0)

    for g in range(LOCAL):
        kv_arrived(kvf, 1, g)
        turn(kvf, g, HEAD_DIM)
    finishes = [forward_part(0)]
    hop_sums(1)
    finishes.append(forward_part(1))

    for g in range(LOCAL):
        own = acc[g, pl.ds(member * rows, rows), :]
        cross = None
        for k in range(1, GROUP):
            one = source(k)

            @pl.when(is_far(one))
            def _():
                grecv[k, g] = jnp.zeros((rows, LANES), bf16)

            @pl.when(jnp.logical_not(is_far(one)))
            def _():
                place = grecv.at[k, g]
                remote(
                    place, place, gr_send.at[g, k], gr_recv.at[g, k], {"ctx": base + one}
                ).wait_recv()

            value = grecv[k, g].astype(f32)
            if k % PAIR == 0:
                own = own + value
            else:
                cross = value if cross is None else cross + value
        gsum[core * LOCAL + g] = own
        gsum[other * LOCAL + g] = cross
    pair_arrived(3, gq_recv)
    columns = [gsum[h, :, :HEAD_DIM] for h in range(KV_HEADS)]
    columns += [gsum[h, :, HEAD_DIM:] for h in range(KV_HEADS)]
    grad_kv = jnp.concatenate(columns, axis=1).astype(bf16)
    grad_normed = mul(grad_kv, wkv[...], NT)
    grad_normed += mul(gq_my[...], wq[:, my_cols], NT)
    grad_normed += mul(gq_recv[...], wq[:, their_cols], NT)
    values, scale = norm(xb[...])
    plain = values * scale
    pushed = gain_v[...].astype(f32) * grad_normed
    grad_in = cot[...].astype(f32) + scale * (
        pushed - plain * jnp.mean(pushed * plain, axis=-1, keepdims=True)
    )
    ob[...] = grad_in.astype(bf16)
    finish_b = shift(rounds, ob, outb_h, before, 0, rows, 0, sections - 1)

    for part in range(2, rounds):
        finishes.append(forward_part(part))

    for copy in pair_copies:
        copy.wait_send()
    finish_kv(kvb, 0)
    finish_kv(kvf, 1)
    for g in range(LOCAL):
        finish_sums(g)
    for finish in finishes:
        finish()
    finish_b()


def shards(fwd_in, bwd_saved, bwd_cot, new_tokens, loss_cot, gain, w_query, w_keyval, w_out):
    section_now = lax.axis_index("section")
    sections = lax.axis_size("section")
    rows, width = fwd_in.shape[1:]
    mem = rows - new_tokens.shape[0]
    both = PAIR * rows
    total = GROUP * rows
    stack = SHARED * both
    half = width // PAIR
    rounds = stack // LANES // UNROLL
    anywhere = pl.BlockSpec(memory_space=pl.ANY)
    far_memory = pl.BlockSpec(memory_space=pltpu.HBM)
    block = jax.ShapeDtypeStruct((rows, width), bf16)
    vmem = pltpu.VMEM
    dma = pltpu.SemaphoreType.DMA
    arrived, returned = pl.pallas_call(
        functools.partial(kernel, sections, mem),
        out_shape=(block, block),
        in_specs=[far_memory] * 7,
        out_specs=(anywhere, anywhere),
        scratch_shapes=[
            vmem((rows, width), bf16), vmem((rows, width), bf16), vmem((rows, width), bf16),
            vmem((1, width), bf16),
            vmem(w_query.shape[1:], bf16), vmem(w_keyval.shape[1:], bf16), vmem(w_out.shape[1:], bf16),
            vmem((rows, width), bf16),
            vmem((LOCAL, total, LANES), bf16), vmem((LOCAL, total, LANES), bf16),
            vmem((LOCAL, HEAD_DIM, total), bf16),
            vmem((LOCAL, stack, LANES), bf16), vmem((LOCAL, stack, LANES), bf16),
            vmem((LOCAL, stack, LANES), bf16),
            vmem((total, LANES), jnp.int32),
            vmem((UNROLL, total, 2 * LANES), f32), vmem((UNROLL, total, LANES), f32),
            vmem((total, UNROLL * 2 * LANES), bf16),
            vmem((LOCAL, total, LANES), f32), vmem((LOCAL, total, LANES), bf16),
            vmem((GROUP, LOCAL, rows, LANES), bf16), vmem((LOCAL, both, LANES), bf16),
            vmem((KV_HEADS, rows, LANES), f32), vmem((2, KV_HEADS, rows, LANES), bf16),
            vmem((3, rows, half), bf16), vmem((3, rows, half), bf16),
            vmem((rows, half), bf16), vmem((rows, half), bf16), vmem((rows, half), bf16),
            vmem((rows, half), bf16), vmem((rows, half), bf16), vmem((rows, half), bf16),
            vmem((rows, width), bf16), vmem((rows, width), bf16),
            dma((7,)), dma((4 + rounds,)), dma((4 + rounds,)),
            dma((2, LOCAL, GROUP)), dma((2, LOCAL, GROUP)),
            dma((LOCAL, GROUP)), dma((LOCAL, GROUP)),
            dma((rounds + 1, 2)), dma((rounds + 1, 2)),
            dma((3, LOCAL)), dma((3, LOCAL)),
        ],
        compiler_params=pltpu.CompilerParams(
            collective_id=0, has_side_effects=True, vmem_limit_bytes=60500 * 1024
        ),
    )(fwd_in[0], bwd_saved[0], bwd_cot[0], gain, w_query[0], w_keyval[0], w_out[0])
    token_row = lax.broadcasted_iota(jnp.int32, (rows, 1), 0) >= mem
    edge = jnp.pad(new_tokens, ((mem, 0), (0, 0)))
    fwd_next = jnp.where(token_row & (section_now == 0), edge, arrived)[None]
    edge = jnp.pad(loss_cot, ((mem, 0), (0, 0)))
    cot_next = jnp.where(token_row & (section_now == sections - 1), edge, returned)[None]
    return (fwd_next, cot_next)


def solution(mesh):
    return jax.shard_map(
        shards,
        mesh=mesh,
        in_specs=(
            P("section", "ctx", None),
            P("section", "ctx", None),
            P("section", "ctx", None),
            P("ctx", None),
            P("ctx", None),
            P("section", None),
            P("section", None, None),
            P("section", None, None),
            P("section", None, None),
        ),
        out_specs=(P("section", "ctx", None), P("section", "ctx", None)),
        check_vma=False,
    )
```

```python
import functools

import jax
import jax.numpy as jnp
from jax import lax
from jax.experimental import pallas as pl
from jax.experimental.pallas import tpu as pltpu
from jax.sharding import PartitionSpec as P

HEADS = 16
KV_HEADS = 4
HEAD_DIM = 64
GROUP = 8
PAIR = 2
CHIPS = GROUP // PAIR
LOCAL = KV_HEADS // PAIR
SHARED = HEADS // KV_HEADS
LANES = 128
PIECES = 4
SPLIT = 2
FOLD = 8
UNROLL = 3

epsilon = 1e-05
far = 1 << 30
wide = 3e38

bf16 = jnp.bfloat16
f32 = jnp.float32
NT = (((1,), (1,)), ((), ()))
NN = (((1,), (0,)), ((), ()))


def mul(a, b, dims=NN):
    return lax.dot_general(a, b, dims, preferred_element_type=f32)


def kernel(
    sections, mem,
    xf_h, xb_h, cot_h, gain_h, wq_h, wkv_h, wo_h,
    outf_h, outb_h,
    xf, xb, cot, gain_v, wq, wkv, wo, normed, kvf, kvb, kvt, qf, qb, gb, bias,
    sd, ex, cat, acc, gsend, grecv, gpass, gsum, kvown, qx_send, qx_recv,
    gq_my, gq_send, gq_recv, mix_my, mix_send, mix_recv, of, ob, via_f, via_b, early,
    local_sem, pair_send, pair_recv, kv_send, kv_recv, gr_send, gr_recv, sec_send, sec_recv,
    hop_send, hop_recv, via_send, via_recv,
):
    rows = xf_h.shape[0]
    width = xf_h.shape[1]
    both = PAIR * rows
    total = GROUP * rows
    half = width // PAIR
    tokens = rows - mem
    slab = LANES // (PAIR * SHARED)
    rounds = rows // slab // UNROLL

    ctx = lax.axis_index("ctx")
    section = lax.axis_index("section")
    member = lax.rem(ctx, GROUP)
    base = ctx - member
    core = lax.rem(member, PAIR)
    chip = member // PAIR
    other = 1 - core
    partner = base + chip * PAIR + other

    after = lax.rem(section + 1, sections)
    before = lax.rem(section + sections - 1, sections)
    barrier = pltpu.get_barrier_semaphore()
    for k in range(1, GROUP):
        pl.semaphore_signal(
            barrier, inc=1, device_id={"ctx": base + lax.rem(member + k, GROUP)},
            device_id_type=pl.DeviceIdType.MESH,
        )
    detour = sections == PAIR * PAIR
    greeted = [after, before]
    if detour:
        greeted.append(lax.rem(section + PAIR, sections))
    for neighbour in greeted:
        pl.semaphore_signal(
            barrier, inc=1, device_id={"section": neighbour},
            device_id_type=pl.DeviceIdType.MESH,
        )

    loads = []
    for at, (src, dst) in enumerate(
        [
            (xb_h, xb), (gain_h, gain_v), (wkv_h, wkv), (wq_h, wq), (xf_h, xf),
            (cot_h, cot), (wo_h, wo),
        ]
    ):
        copy = pltpu.make_async_copy(src, dst, local_sem.at[at])
        copy.start()
        loads.append(copy)
    load_xb, load_gain, load_wkv, load_wq, load_xf, load_cot, load_wo = loads

    def remote(src, dst, send, recv, where):
        return pltpu.make_async_remote_copy(
            src_ref=src, dst_ref=dst, send_sem=send, recv_sem=recv,
            device_id=where, device_id_type=pl.DeviceIdType.MESH,
        )

    pair_copies = []

    def pair_copy(at, src, dst):
        copy = remote(src, dst, pair_send.at[at], pair_recv.at[at], {"ctx": partner})
        copy.start()
        pair_copies.append(copy)

    def pair_arrived(at, dst):
        remote(dst, dst, pair_send.at[at], pair_recv.at[at], {"ctx": partner}).wait_recv()

    def norm(x):
        values = x.astype(f32)
        scale = lax.rsqrt(jnp.mean(values * values, axis=-1, keepdims=True) + epsilon)
        return values, scale

    def make_normed(x_ref):
        values, scale = norm(x_ref[...])
        normed[...] = (values * scale * gain_v[...].astype(f32)).astype(bf16)

    last = CHIPS - 1
    is_end = jnp.logical_or(chip == 0, chip == last)
    is_middle = jnp.logical_not(is_end)
    opposite = last - chip
    nearest_end = jnp.where(chip == 1, 0, last)
    adjacent = jnp.where(is_end, jnp.where(chip == 0, 1, last - 1), nearest_end)
    hop_at = jnp.where(chip == 0, last - 1, 1)
    hop_from = jnp.where(chip == 1, last, 0)
    hop_to = last - hop_from
    sum_via = jnp.where(chip == 0, 1, last - 1)
    sum_from = jnp.where(chip == 1, 0, last)

    def peer(k):
        return lax.rem(member + k, GROUP)

    def source(k):
        return lax.rem(member + GROUP - k, GROUP)

    def is_far(one):
        return jnp.logical_and(is_end, one // PAIR == opposite)

    order = sorted(range(1, GROUP), key=lambda k: abs(k - GROUP // 2))

    def project_kv(kv_ref, kind):
        keyval = mul(normed[...], wkv[...])
        for h in range(KV_HEADS):
            at = h * HEAD_DIM
            after_keys = KV_HEADS * HEAD_DIM + at
            kvown[kind, h] = jnp.concatenate(
                [keyval[:, at : at + HEAD_DIM], keyval[:, after_keys : after_keys + HEAD_DIM]],
                axis=1,
            ).astype(bf16)
        for g in range(LOCAL):
            kv_ref[g, pl.ds(member * rows, rows), :] = kvown[kind, core * LOCAL + g]

    def kv_copy(kv_ref, kind, g, k):
        to = peer(k)
        return remote(
            kvown.at[kind, lax.rem(to, PAIR) * LOCAL + g],
            kv_ref.at[g, pl.ds(member * rows, rows)],
            kv_send.at[kind, g, k], kv_recv.at[kind, g, k], {"ctx": base + to},
        )

    def is_first(one):
        away = one // PAIR
        ends = jnp.logical_and(is_end, jnp.logical_or(away == hop_at, away == chip))
        return jnp.logical_or(ends, jnp.logical_and(is_middle, away == adjacent))

    def send_kv(kv_ref, kind, g, phase=None):
        for k in order:
            use = jnp.logical_not(is_far(peer(k)))
            if phase is not None:
                first = is_first(peer(k))
                use = jnp.logical_and(use, first if phase == 0 else jnp.logical_not(first))

            @pl.when(use)
            def _():
                kv_copy(kv_ref, kind, g, k).start()

    def finish_kv(kv_ref, kind):
        for g in range(LOCAL):
            for k in order:
                @pl.when(jnp.logical_not(is_far(peer(k))))
                def _():
                    kv_copy(kv_ref, kind, g, k).wait_send()

            @pl.when(is_middle)
            def _():
                hop_copy(kv_ref, kind, g).wait_send()

    def hop_copy(kv_ref, kind, g):
        place = kv_ref.at[g, pl.ds(hop_from * both, both)]
        return remote(
            place, place, hop_send.at[kind, g], hop_recv.at[kind, g],
            {"ctx": base + hop_to * PAIR + core},
        )

    def kv_wait(kv_ref, kind, g, one):
        k = lax.rem(member + GROUP - one, GROUP)
        place = kv_ref.at[g, pl.ds(one * rows, rows)]
        remote(
            place, place, kv_send.at[kind, g, k], kv_recv.at[kind, g, k], {"ctx": base + one}
        ).wait_recv()

    def hop_kv(kv_ref, kind, g):
        @pl.when(is_middle)
        def _():
            for c in range(PAIR):
                kv_wait(kv_ref, kind, g, hop_from * PAIR + c)
            hop_copy(kv_ref, kind, g).start()

    def near_kv(kv_ref, kind, g):
        @pl.when(is_end)
        def _():
            for c in range(PAIR):
                kv_wait(kv_ref, kind, g, adjacent * PAIR + c)

    def kv_arrived(kv_ref, kind, g, near_done=False):
        for k in range(1, GROUP):
            one = source(k)
            done = jnp.logical_and(is_middle, one // PAIR == hop_from)
            if near_done:
                done = jnp.logical_or(done, jnp.logical_and(is_end, one // PAIR == adjacent))

            @pl.when(jnp.logical_not(jnp.logical_or(is_far(one), done)))
            def _():
                kv_wait(kv_ref, kind, g, one)

        @pl.when(is_end)
        def _():
            place = kv_ref.at[g, pl.ds(opposite * both, both)]
            remote(
                place, place, hop_send.at[kind, g], hop_recv.at[kind, g],
                {"ctx": base + opposite * PAIR + core},
            ).wait_recv()

    def gr_copy(g, k):
        to = peer(k)
        return remote(
            gsend.at[g, pl.ds(to * rows, rows)], grecv.at[k, g],
            gr_send.at[g, k], gr_recv.at[g, k], {"ctx": base + to},
        )

    def is_summed(one):
        return jnp.logical_and(is_middle, one // PAIR == last - sum_from)

    def sum_copy(g, where):
        return remote(
            gsend.at[g, pl.ds(opposite * both, both)], gpass.at[g],
            hop_send.at[2, g], hop_recv.at[2, g], {"ctx": base + where * PAIR + core},
        )

    def send_sums(g):
        gsend[g] = acc[g].astype(bf16)

        @pl.when(is_end)
        def _():
            sum_copy(g, sum_via).start()

        for k in order:
            to = peer(k)

            @pl.when(jnp.logical_not(jnp.logical_or(is_far(to), is_summed(to))))
            def _():
                gr_copy(g, k).start()

    def hop_sums(g):
        @pl.when(is_middle)
        def _():
            sum_copy(g, sum_from).wait_recv()
            place = pl.ds((last - sum_from) * both, both)
            gsend[g, place, :] = (acc[g, place, :] + gpass[g].astype(f32)).astype(bf16)
            for k in order:
                @pl.when(is_summed(peer(k)))
                def _():
                    gr_copy(g, k).start()

    def finish_sums(g):
        @pl.when(is_end)
        def _():
            sum_copy(g, sum_via).wait_send()

        for k in order:
            @pl.when(jnp.logical_not(is_far(peer(k))))
            def _():
                gr_copy(g, k).wait_send()

    def spread(matrix, dst, block, upper, factor):
        rounded = matrix.astype(f32) * factor
        zero = jnp.zeros((rows, HEAD_DIM), f32)
        for g in range(LOCAL):
            for h in range(SHARED):
                at = (g * SHARED + h) * HEAD_DIM
                piece = rounded[:, at : at + HEAD_DIM]
                parts = [zero, piece] if upper else [piece, zero]
                wide = jnp.concatenate(parts, axis=1).astype(bf16)
                for i in range(rows // slab):
                    to = i * LANES + (block * SHARED + h) * slab
                    dst[g, to : to + slab, :] = wide[i * slab : (i + 1) * slab, :]

    scale_by = HEAD_DIM ** (-0.5)
    my_cols = pl.ds(pl.multiple_of(core * half, half), half)
    their_cols = pl.ds(pl.multiple_of(other * half, half), half)

    def make_query(at, q_ref):
        qx_send[at] = mul(normed[...], wq[:, their_cols]).astype(bf16)
        spread(mul(normed[...], wq[:, my_cols]).astype(bf16), q_ref, 0, False, scale_by)

    big = total // PIECES
    step = big // SPLIT

    def make_bias():
        lane = lax.broadcasted_iota(jnp.int32, (1, LANES), 1)
        block = jnp.where(lane < LANES // PAIR, member, chip * PAIR + other)
        key = lax.broadcasted_iota(jnp.int32, (rows, LANES), 0)
        for i in range(rows // slab):
            inner = i * slab + lax.rem(lane, slab)
            position = jnp.where(inner < mem, far, block * tokens + inner - mem)
            for b in range(GROUP):
                place = jnp.where(key < mem, -1, b * tokens + key - mem)
                bias[i, b * rows : (b + 1) * rows, :] = jnp.where(place <= position, wide, -1e30)

    parts = [slice(p * step, (p + 1) * step) for p in range(PIECES * SPLIT)]

    load_xb.wait()
    load_gain.wait()
    make_normed(xb)
    load_wkv.wait()
    project_kv(kvb, 0)
    pl.semaphore_wait(barrier, GROUP - 1 + len(greeted))
    send_kv(kvb, 0, 0, 0)
    load_wq.wait()
    make_query(0, qb)
    send_kv(kvb, 0, 0, 1)
    pair_copy(0, qx_send.at[0], qx_recv.at[0])
    load_cot.wait()
    load_wo.wait()
    qx_send[2] = mul(cot[...], wo[their_cols, :], NT).astype(bf16)
    pair_copy(2, qx_send.at[2], qx_recv.at[2])
    spread(mul(cot[...], wo[my_cols, :], NT).astype(bf16), gb, 0, True, 1.0)
    load_xf.wait()
    make_normed(xf)
    project_kv(kvf, 1)
    pair_arrived(0, qx_recv.at[0])
    spread(qx_recv[0], qb, 1, False, scale_by)
    pair_arrived(2, qx_recv.at[2])
    spread(qx_recv[2], gb, 1, True, 1.0)
    near_kv(kvb, 0, 0)
    hop_kv(kvb, 0, 0)
    send_kv(kvb, 0, 1)
    make_query(1, qf)
    pair_copy(1, qx_send.at[1], qx_recv.at[1])
    make_bias()

    def put_heads(g, i, turned, mine_ref, theirs_ref):
        place = pl.ds(pl.multiple_of(i * slab, slab), slab)
        for block, ref in enumerate((mine_ref, theirs_ref)):
            for h in range(0, SHARED, 2):
                at = (block * SHARED + h) * slab
                pair = jnp.concatenate(
                    [turned[at : at + slab, :], turned[at + slab : at + 2 * slab, :]], axis=1
                )
                to = pl.multiple_of((g * SHARED + h) * HEAD_DIM, LANES)
                ref[place, pl.ds(to, LANES)] = pair.astype(bf16)

    def folded(x):
        return x.reshape(step // FOLD, FOLD, LANES)

    def combine(tops, sums):
        top = functools.reduce(jnp.maximum, tops)
        top = jnp.max(top, axis=0, keepdims=True)
        weights = [jnp.exp(t - top) for t in tops]
        norm_sum = sum(w * s for w, s in zip(weights, sums))
        return weights, 1.0 / jnp.sum(norm_sum, axis=0, keepdims=True)

    def backward_chunk(g, chunks):
        starts = [pl.multiple_of(i * LANES, LANES) for i in chunks]
        pairs = [
            jnp.concatenate([qb[g, pl.ds(at, LANES), :], gb[g, pl.ds(at, LANES), :]], axis=0)
            for at in starts
        ]
        for u, i in enumerate(chunks):
            tops, sums, dots = [], [], []
            products = [
                mul(kvb[g, p * big : (p + 1) * big, :], pairs[u], NT) for p in range(PIECES)
            ]
            for at, part in enumerate(parts):
                within = at % SPLIT * step
                product = products[at // SPLIT][within : within + step, :]
                scores = folded(jnp.minimum(product[:, :LANES], bias[i, part, :]))
                top = jnp.max(scores, axis=0)
                expd = jnp.exp(scores - top)
                rates = folded(product[:, LANES:])
                ex[u, part, :] = expd.reshape(step, LANES)
                sd[u, part, :] = rates.reshape(step, LANES)
                tops.append(top)
                sums.append(jnp.sum(expd, axis=0))
                dots.append(jnp.sum(expd * rates, axis=0))
            weights, inverse = combine(tops, sums)
            delta = sum(w * d for w, d in zip(weights, dots))
            delta = jnp.sum(delta, axis=0, keepdims=True) * inverse
            at = u * 2 * LANES
            for part, weight in zip(parts, weights):
                probs = folded(ex[u, part, :]) * (weight * inverse)
                dscores = probs * (folded(sd[u, part, :]) - delta)
                cat[part, at + LANES : at + 2 * LANES] = probs.reshape(step, LANES).astype(bf16)
                cat[part, at : at + LANES] = dscores.reshape(step, LANES).astype(bf16)
        everything = jnp.concatenate(pairs, axis=0)
        for part in parts:
            acc[g, part, :] += mul(cat[part, :], everything)
        for u, i in enumerate(chunks):
            at = u * 2 * LANES
            turned = mul(kvt[g], cat[:, at : at + LANES])
            put_heads(g, i, turned.T * scale_by, gq_my, gq_send)

    def forward_chunk(g, chunks):
        for u, i in enumerate(chunks):
            start = pl.multiple_of(i * LANES, LANES)
            queries = qf[g, pl.ds(start, LANES), :]
            tops, sums = [], []
            products = [
                mul(kvf[g, p * big : (p + 1) * big, :], queries, NT) for p in range(PIECES)
            ]
            for at, part in enumerate(parts):
                within = at % SPLIT * step
                product = products[at // SPLIT][within : within + step, :]
                scores = folded(jnp.minimum(product, bias[i, part, :]))
                top = jnp.max(scores, axis=0)
                expd = jnp.exp(scores - top)
                ex[u, part, :] = expd.reshape(step, LANES)
                tops.append(top)
                sums.append(jnp.sum(expd, axis=0))
            weights, inverse = combine(tops, sums)
            for part, weight in zip(parts, weights):
                probs = folded(ex[u, part, :]) * (weight * inverse)
                cat[part, u * LANES : (u + 1) * LANES] = probs.reshape(step, LANES).astype(bf16)
        turned = mul(kvt[g], cat[:, : len(chunks) * LANES])
        for u, i in enumerate(chunks):
            put_heads(g, i, turned[:, u * LANES : (u + 1) * LANES].T, mix_my, mix_send)

    def run(chunk, g, begin, end, actions):
        def body(i, carry):
            for at, action in actions.items():
                pl.when(i == at)(action)
            chunk(g, [i * UNROLL + u for u in range(UNROLL)])
            return carry

        lax.fori_loop(begin, end, body, 0)

    def turn(kv_ref, g, first):
        whole = kv_ref[g].astype(f32).T
        kvt[g] = whole[first : first + HEAD_DIM, :].astype(bf16)

    def after_first():
        hop_kv(kvf, 1, 0)
        send_kv(kvf, 1, 1)

    def at_start():
        hop_kv(kvb, 0, 1)
        send_kv(kvf, 1, 0)

    backward_actions = [
        {0: at_start, 2: after_first},
        {1: lambda: hop_kv(kvf, 1, 1), 2: lambda: hop_sums(0)},
    ]
    for g in range(LOCAL):
        kv_arrived(kvb, 0, g, g == 0)
        turn(kvb, g, 0)
        acc[g] = jnp.zeros((total, LANES), f32)
        run(backward_chunk, g, 0, rounds, backward_actions[g])
        send_sums(g)
    pair_copy(3, gq_send, gq_recv)
    pair_arrived(1, qx_recv.at[1])
    spread(qx_recv[1], qf, 1, False, scale_by)

    def shift(at, src, dst, via, where, begin, end, edge, arrive_edge, turning, target):
        place = pl.ds(max(begin, mem), end - max(begin, mem))

        def copy(index, one):
            return remote(
                src.at[one], dst.at[one],
                sec_send.at[at, index], sec_recv.at[at, index], {"section": where},
            )

        small = copy(0, pl.ds(begin, mem - begin)) if begin < mem else None
        large = copy(1, place)
        around = remote(
            src.at[place], via.at[place], via_send.at[at], via_recv.at[at], {"section": edge}
        )
        onward = remote(
            via.at[place], dst.at[place],
            sec_send.at[at, 1], sec_recv.at[at, 1], {"section": target},
        )
        if detour:
            turns = jnp.logical_and(section == turning, core == 1)
            passes = jnp.logical_and(section == edge, core == 1)
        if small is not None:
            small.start()
        straight = section != edge
        if detour:
            straight = jnp.logical_and(straight, jnp.logical_not(turns))

            @pl.when(turns)
            def _():
                around.start()

        @pl.when(straight)
        def _():
            large.start()

        def pass_on():
            if detour:
                @pl.when(passes)
                def _():
                    around.wait_recv()
                    onward.start()

        def finish():
            if small is not None:
                small.wait()

            if detour:
                @pl.when(turns)
                def _():
                    around.wait_send()

                @pl.when(passes)
                def _():
                    onward.wait_send()

            @pl.when(straight)
            def _():
                large.wait_send()

            @pl.when(section != arrive_edge)
            def _():
                large.wait_recv()

        return pass_on, finish

    def attend(g, at):
        forward_chunk(g, [at * UNROLL + u for u in range(UNROLL)])
        if g == LOCAL - 1:
            place = slice(at * UNROLL * slab, (at + 1) * UNROLL * slab)
            pair_copy(4 + at, mix_send.at[place], mix_recv.at[place])

    def project_out(at):
        begin, end = at * UNROLL * slab, (at + 1) * UNROLL * slab
        place = slice(begin, end)
        made = xf[place, :].astype(f32) + mul(mix_my[place, :], wo[my_cols, :])
        pair_arrived(4 + at, mix_recv.at[place])
        made += mul(mix_recv[place, :], wo[their_cols, :])
        of[place, :] = made.astype(bf16)
        return shift(
            at, of, outf_h, via_f, after, begin, end, sections - 1, 0,
            sections // PAIR - 1, sections // PAIR,
        )

    kv_arrived(kvf, 1, 0)
    turn(kvf, 0, HEAD_DIM)
    attend(0, 0)
    attend(0, 1)
    kv_arrived(kvf, 1, 1)
    turn(kvf, 1, HEAD_DIM)
    attend(1, 0)
    hop_sums(1)
    pair_arrived(3, gq_recv)
    early[...] = mul(gq_my[...], wq[:, my_cols], NT) + mul(gq_recv[...], wq[:, their_cols], NT)
    moves = [project_out(0)]
    attend(1, 1)
    attend(0, 2)
    moves[0][0]()
    moves.append(project_out(1))

    for g in range(LOCAL):
        own = acc[g, pl.ds(member * rows, rows), :]
        cross = None
        for k in range(1, GROUP):
            one = source(k)

            @pl.when(is_far(one))
            def _():
                grecv[k, g] = jnp.zeros((rows, LANES), bf16)

            @pl.when(jnp.logical_not(is_far(one)))
            def _():
                place = grecv.at[k, g]
                remote(
                    place, place, gr_send.at[g, k], gr_recv.at[g, k], {"ctx": base + one}
                ).wait_recv()

            value = grecv[k, g].astype(f32)
            if k % PAIR == 0:
                own = own + value
            else:
                cross = value if cross is None else cross + value
        gsum[core * LOCAL + g] = own
        gsum[other * LOCAL + g] = cross
    columns = [gsum[h, :, :HEAD_DIM] for h in range(KV_HEADS)]
    columns += [gsum[h, :, HEAD_DIM:] for h in range(KV_HEADS)]
    grad_kv = jnp.concatenate(columns, axis=1).astype(bf16)
    grad_normed = early[...] + mul(grad_kv, wkv[...], NT)
    values, scale = norm(xb[...])
    plain = values * scale
    pushed = gain_v[...].astype(f32) * grad_normed
    grad_in = cot[...].astype(f32) + scale * (
        pushed - plain * jnp.mean(pushed * plain, axis=-1, keepdims=True)
    )
    ob[...] = grad_in.astype(bf16)
    backs = [
        shift(
            rounds + p, ob, outb_h, via_b, before, p * UNROLL * slab, (p + 1) * UNROLL * slab,
            0, sections - 1, sections // PAIR, sections // PAIR - 1,
        )
        for p in range(rounds)
    ]
    attend(1, 2)
    moves[1][0]()
    moves.append(project_out(2))
    for pass_on, _ in backs:
        pass_on()
    moves[2][0]()
    moves += backs

    for copy in pair_copies:
        copy.wait_send()
    finish_kv(kvb, 0)
    finish_kv(kvf, 1)
    for g in range(LOCAL):
        finish_sums(g)
    for _, finish in moves:
        finish()


def shards(fwd_in, bwd_saved, bwd_cot, new_tokens, loss_cot, gain, w_query, w_keyval, w_out):
    section_now = lax.axis_index("section")
    sections = lax.axis_size("section")
    rows, width = fwd_in.shape[1:]
    mem = rows - new_tokens.shape[0]
    both = PAIR * rows
    total = GROUP * rows
    stack = SHARED * both
    half = width // PAIR
    rounds = stack // LANES // UNROLL
    anywhere = pl.BlockSpec(memory_space=pl.ANY)
    far_memory = pl.BlockSpec(memory_space=pltpu.HBM)
    block = jax.ShapeDtypeStruct((rows, width), bf16)
    vmem = pltpu.VMEM
    dma = pltpu.SemaphoreType.DMA
    arrived, returned = pl.pallas_call(
        functools.partial(kernel, sections, mem),
        out_shape=(block, block),
        in_specs=[far_memory] * 7,
        out_specs=(anywhere, anywhere),
        scratch_shapes=[
            vmem((rows, width), bf16), vmem((rows, width), bf16), vmem((rows, width), bf16),
            vmem((1, width), bf16),
            vmem(w_query.shape[1:], bf16), vmem(w_keyval.shape[1:], bf16), vmem(w_out.shape[1:], bf16),
            vmem((rows, width), bf16),
            vmem((LOCAL, total, LANES), bf16), vmem((LOCAL, total, LANES), bf16),
            vmem((LOCAL, HEAD_DIM, total), bf16),
            vmem((LOCAL, stack, LANES), bf16), vmem((LOCAL, stack, LANES), bf16),
            vmem((LOCAL, stack, LANES), bf16),
            vmem((rows * PAIR * SHARED // LANES, total, LANES), f32),
            vmem((UNROLL, total, LANES), f32), vmem((UNROLL, total, LANES), f32),
            vmem((total, UNROLL * 2 * LANES), bf16),
            vmem((LOCAL, total, LANES), f32), vmem((LOCAL, total, LANES), bf16),
            vmem((GROUP, LOCAL, rows, LANES), bf16), vmem((LOCAL, both, LANES), bf16),
            vmem((KV_HEADS, rows, LANES), f32), vmem((2, KV_HEADS, rows, LANES), bf16),
            vmem((3, rows, half), bf16), vmem((3, rows, half), bf16),
            vmem((rows, half), bf16), vmem((rows, half), bf16), vmem((rows, half), bf16),
            vmem((rows, half), bf16), vmem((rows, half), bf16), vmem((rows, half), bf16),
            vmem((rows, width), bf16), vmem((rows, width), bf16),
            vmem((rows, width), bf16), vmem((rows, width), bf16), vmem((rows, width), f32),
            dma((7,)), dma((4 + rounds,)), dma((4 + rounds,)),
            dma((2, LOCAL, GROUP)), dma((2, LOCAL, GROUP)),
            dma((LOCAL, GROUP)), dma((LOCAL, GROUP)),
            dma((2 * rounds, 2)), dma((2 * rounds, 2)),
            dma((3, LOCAL)), dma((3, LOCAL)),
            dma((2 * rounds,)), dma((2 * rounds,)),
        ],
        compiler_params=pltpu.CompilerParams(
            collective_id=0, has_side_effects=True, vmem_limit_bytes=54500 * 1024
        ),
    )(fwd_in[0], bwd_saved[0], bwd_cot[0], gain, w_query[0], w_keyval[0], w_out[0])
    token_row = lax.broadcasted_iota(jnp.int32, (rows, 1), 0) >= mem
    edge = jnp.pad(new_tokens, ((mem, 0), (0, 0)))
    fwd_next = jnp.where(token_row & (section_now == 0), edge, arrived)[None]
    edge = jnp.pad(loss_cot, ((mem, 0), (0, 0)))
    cot_next = jnp.where(token_row & (section_now == sections - 1), edge, returned)[None]
    return (fwd_next, cot_next)


def solution(mesh):
    return jax.shard_map(
        shards,
        mesh=mesh,
        in_specs=(
            P("section", "ctx", None),
            P("section", "ctx", None),
            P("section", "ctx", None),
            P("ctx", None),
            P("ctx", None),
            P("section", None),
            P("section", None, None),
            P("section", None, None),
            P("section", None, None),
        ),
        out_specs=(P("section", "ctx", None), P("section", "ctx", None)),
        check_vma=False,
    )
```

```python
import functools

import jax
import jax.numpy as jnp
from jax import lax
from jax.experimental import pallas as pl
from jax.experimental.pallas import tpu as pltpu
from jax.sharding import PartitionSpec as P

HEADS = 16
KV_HEADS = 4
HEAD_DIM = 64
GROUP = 8
PAIR = 2
CHIPS = GROUP // PAIR
LOCAL = KV_HEADS // PAIR
SHARED = HEADS // KV_HEADS
LANES = 128
PIECES = 4
SPLIT = 2
FOLD = 8
UNROLL = 3

epsilon = 1e-05
far = 1 << 30
wide = 3e38

bf16 = jnp.bfloat16
f32 = jnp.float32
NT = (((1,), (1,)), ((), ()))
NN = (((1,), (0,)), ((), ()))


def mul(a, b, dims=NN):
    return lax.dot_general(a, b, dims, preferred_element_type=f32)


def kernel(
    sections, mem,
    xf_h, xb_h, cot_h, gain_h, wq_h, wkv_h, wo_h,
    outf_h, outb_h,
    xf, xb, cot, gain_v, wq, wkv, wo, normed, kvf, kvb, kvt, qf, qb, gb, bias,
    sd, ex, cat, acc, gsend, grecv, gpass, gsum, kvown, qx_send, qx_recv,
    gq_my, gq_send, gq_recv, mix_my, mix_send, mix_recv, of, ob, via_f, via_b, early,
    local_sem, pair_send, pair_recv, kv_send, kv_recv, gr_send, gr_recv, sec_send, sec_recv,
    hop_send, hop_recv, via_send, via_recv,
):
    rows = xf_h.shape[0]
    width = xf_h.shape[1]
    both = PAIR * rows
    total = GROUP * rows
    half = width // PAIR
    tokens = rows - mem
    slab = LANES // (PAIR * SHARED)
    rounds = rows // slab // UNROLL

    ctx = lax.axis_index("ctx")
    section = lax.axis_index("section")
    member = lax.rem(ctx, GROUP)
    base = ctx - member
    core = lax.rem(member, PAIR)
    chip = member // PAIR
    other = 1 - core
    partner = base + chip * PAIR + other

    after = lax.rem(section + 1, sections)
    before = lax.rem(section + sections - 1, sections)
    barrier = pltpu.get_barrier_semaphore()
    for k in range(1, GROUP):
        pl.semaphore_signal(
            barrier, inc=1, device_id={"ctx": base + lax.rem(member + k, GROUP)},
            device_id_type=pl.DeviceIdType.MESH,
        )
    detour = sections == PAIR * PAIR
    greeted = [after, before]
    if detour:
        greeted.append(lax.rem(section + PAIR, sections))
    for neighbour in greeted:
        pl.semaphore_signal(
            barrier, inc=1, device_id={"section": neighbour},
            device_id_type=pl.DeviceIdType.MESH,
        )

    loads = []
    for at, (src, dst) in enumerate(
        [
            (xb_h, xb), (gain_h, gain_v), (wkv_h, wkv), (wq_h, wq), (xf_h, xf),
            (cot_h, cot), (wo_h, wo),
        ]
    ):
        copy = pltpu.make_async_copy(src, dst, local_sem.at[at])
        copy.start()
        loads.append(copy)
    load_xb, load_gain, load_wkv, load_wq, load_xf, load_cot, load_wo = loads

    def remote(src, dst, send, recv, where):
        return pltpu.make_async_remote_copy(
            src_ref=src, dst_ref=dst, send_sem=send, recv_sem=recv,
            device_id=where, device_id_type=pl.DeviceIdType.MESH,
        )

    pair_copies = []

    def pair_copy(at, src, dst):
        copy = remote(src, dst, pair_send.at[at], pair_recv.at[at], {"ctx": partner})
        copy.start()
        pair_copies.append(copy)

    def pair_arrived(at, dst):
        remote(dst, dst, pair_send.at[at], pair_recv.at[at], {"ctx": partner}).wait_recv()

    def norm(x):
        values = x.astype(f32)
        scale = lax.rsqrt(jnp.mean(values * values, axis=-1, keepdims=True) + epsilon)
        return values, scale

    def make_normed(x_ref):
        values, scale = norm(x_ref[...])
        normed[...] = (values * scale * gain_v[...].astype(f32)).astype(bf16)

    last = CHIPS - 1
    is_end = jnp.logical_or(chip == 0, chip == last)
    is_middle = jnp.logical_not(is_end)
    opposite = last - chip
    nearest_end = jnp.where(chip == 1, 0, last)
    adjacent = jnp.where(is_end, jnp.where(chip == 0, 1, last - 1), nearest_end)
    hop_at = jnp.where(chip == 0, last - 1, 1)
    hop_from = jnp.where(chip == 1, last, 0)
    hop_to = last - hop_from
    sum_via = jnp.where(chip == 0, 1, last - 1)
    sum_from = jnp.where(chip == 1, 0, last)

    def peer(k):
        return lax.rem(member + k, GROUP)

    def source(k):
        return lax.rem(member + GROUP - k, GROUP)

    def is_far(one):
        return jnp.logical_and(is_end, one // PAIR == opposite)

    order = sorted(range(1, GROUP), key=lambda k: abs(k - GROUP // 2))

    def project_kv(kv_ref, kind):
        keyval = mul(normed[...], wkv[...])
        for h in range(KV_HEADS):
            at = h * HEAD_DIM
            after_keys = KV_HEADS * HEAD_DIM + at
            kvown[kind, h] = jnp.concatenate(
                [keyval[:, at : at + HEAD_DIM], keyval[:, after_keys : after_keys + HEAD_DIM]],
                axis=1,
            ).astype(bf16)
        for g in range(LOCAL):
            kv_ref[g, pl.ds(member * rows, rows), :] = kvown[kind, core * LOCAL + g]

    def early_class(src, dst):
        ends = jnp.logical_or(dst == 0, dst == last)
        near = jnp.where(dst == 0, 1, last - 1)
        across = jnp.where(dst == 1, last, 0)
        return jnp.where(src == jnp.where(ends, near, across), 1, 0)

    def kv_copy(kv_ref, kind, g, k):
        to = peer(k)
        return remote(
            kvown.at[kind, lax.rem(to, PAIR) * LOCAL + g],
            kv_ref.at[g, pl.ds(member * rows, rows)],
            kv_send.at[kind, g], kv_recv.at[kind, g, early_class(chip, to // PAIR)],
            {"ctx": base + to},
        )

    def is_first(one):
        away = one // PAIR
        ends = jnp.logical_and(is_end, jnp.logical_or(away == hop_at, away == chip))
        return jnp.logical_or(ends, jnp.logical_and(is_middle, away == adjacent))

    def send_kv(kv_ref, kind, g, phase=None):
        for k in order:
            use = jnp.logical_not(is_far(peer(k)))
            if phase is not None:
                first = is_first(peer(k))
                use = jnp.logical_and(use, first if phase == 0 else jnp.logical_not(first))

            @pl.when(use)
            def _():
                kv_copy(kv_ref, kind, g, k).start()

    def by_place(at_end, at_middle, action):
        pl.when(is_end)(lambda: action(at_end))
        pl.when(is_middle)(lambda: action(at_middle))

    def finish_kv(kv_ref, kind):
        for g in range(LOCAL):
            def wait(count):
                place = kv_ref.at[g, pl.ds(0, count * rows)]
                remote(
                    place, place, kv_send.at[kind, g], kv_recv.at[kind, g, 0], {"ctx": partner}
                ).wait_send()

            by_place(GROUP - 1 - PAIR, GROUP - 1, wait)

            @pl.when(is_middle)
            def _():
                hop_copy(kv_ref, kind, g).wait_send()

    def hop_copy(kv_ref, kind, g):
        place = kv_ref.at[g, pl.ds(hop_from * both, both)]
        return remote(
            place, place, hop_send.at[kind, g], hop_recv.at[kind, g],
            {"ctx": base + hop_to * PAIR + core},
        )

    def kv_wait(kv_ref, kind, g, which, count):
        place = kv_ref.at[g, pl.ds(0, count * rows)]
        remote(
            place, place, kv_send.at[kind, g], kv_recv.at[kind, g, which], {"ctx": partner}
        ).wait_recv()

    def hop_kv(kv_ref, kind, g):
        @pl.when(is_middle)
        def _():
            kv_wait(kv_ref, kind, g, 1, PAIR)
            hop_copy(kv_ref, kind, g).start()

    def near_kv(kv_ref, kind, g):
        @pl.when(is_end)
        def _():
            kv_wait(kv_ref, kind, g, 1, PAIR)

    def kv_arrived(kv_ref, kind, g, near_done=False):
        by_place(
            GROUP - 1 - 2 * PAIR, GROUP - 1 - PAIR,
            lambda count: kv_wait(kv_ref, kind, g, 0, count),
        )
        if not near_done:
            near_kv(kv_ref, kind, g)

        @pl.when(is_end)
        def _():
            place = kv_ref.at[g, pl.ds(opposite * both, both)]
            remote(
                place, place, hop_send.at[kind, g], hop_recv.at[kind, g],
                {"ctx": base + opposite * PAIR + core},
            ).wait_recv()

    def gr_copy(g, k):
        to = peer(k)
        return remote(
            gsend.at[g, pl.ds(to * rows, rows)], grecv.at[k, g],
            gr_send.at[g], gr_recv.at[g], {"ctx": base + to},
        )

    def is_summed(one):
        return jnp.logical_and(is_middle, one // PAIR == last - sum_from)

    def sum_copy(g, where):
        return remote(
            gsend.at[g, pl.ds(opposite * both, both)], gpass.at[g],
            hop_send.at[2, g], hop_recv.at[2, g], {"ctx": base + where * PAIR + core},
        )

    def send_sums(g):
        gsend[g] = acc[g].astype(bf16)

        @pl.when(is_end)
        def _():
            sum_copy(g, sum_via).start()

        for k in order:
            to = peer(k)

            @pl.when(jnp.logical_not(jnp.logical_or(is_far(to), is_summed(to))))
            def _():
                gr_copy(g, k).start()

    def hop_sums(g):
        @pl.when(is_middle)
        def _():
            sum_copy(g, sum_from).wait_recv()
            place = pl.ds((last - sum_from) * both, both)
            gsend[g, place, :] = (acc[g, place, :] + gpass[g].astype(f32)).astype(bf16)
            for k in order:
                @pl.when(is_summed(peer(k)))
                def _():
                    gr_copy(g, k).start()

    def finish_sums(g):
        @pl.when(is_end)
        def _():
            sum_copy(g, sum_via).wait_send()

        def wait(count):
            place = gsend.at[g, pl.ds(0, count * rows)]
            remote(place, place, gr_send.at[g], gr_recv.at[g], {"ctx": partner}).wait_send()

        by_place(GROUP - 1 - PAIR, GROUP - 1, wait)

    def spread(matrix, dst, block, upper, factor):
        rounded = matrix.astype(f32) * factor
        zero = jnp.zeros((rows, HEAD_DIM), f32)
        for g in range(LOCAL):
            for h in range(SHARED):
                at = (g * SHARED + h) * HEAD_DIM
                piece = rounded[:, at : at + HEAD_DIM]
                parts = [zero, piece] if upper else [piece, zero]
                wide = jnp.concatenate(parts, axis=1).astype(bf16)
                for i in range(rows // slab):
                    to = i * LANES + (block * SHARED + h) * slab
                    dst[g, to : to + slab, :] = wide[i * slab : (i + 1) * slab, :]

    scale_by = HEAD_DIM ** (-0.5)
    my_cols = pl.ds(pl.multiple_of(core * half, half), half)
    their_cols = pl.ds(pl.multiple_of(other * half, half), half)

    def make_query(at, q_ref):
        qx_send[at] = mul(normed[...], wq[:, their_cols]).astype(bf16)
        spread(mul(normed[...], wq[:, my_cols]).astype(bf16), q_ref, 0, False, scale_by)

    big = total // PIECES
    step = big // SPLIT

    def make_bias():
        lane = lax.broadcasted_iota(jnp.int32, (1, LANES), 1)
        block = jnp.where(lane < LANES // PAIR, member, chip * PAIR + other)
        key = lax.broadcasted_iota(jnp.int32, (rows, LANES), 0)
        for i in range(rows // slab):
            inner = i * slab + lax.rem(lane, slab)
            position = jnp.where(inner < mem, far, block * tokens + inner - mem)
            for b in range(GROUP):
                place = jnp.where(key < mem, -1, b * tokens + key - mem)
                bias[i, b * rows : (b + 1) * rows, :] = jnp.where(place <= position, wide, -1e30)

    parts = [slice(p * step, (p + 1) * step) for p in range(PIECES * SPLIT)]

    load_xb.wait()
    load_gain.wait()
    make_normed(xb)
    load_wkv.wait()
    project_kv(kvb, 0)
    pl.semaphore_wait(barrier, GROUP - 1 + len(greeted))
    send_kv(kvb, 0, 0, 0)
    load_wq.wait()
    make_query(0, qb)
    send_kv(kvb, 0, 0, 1)
    pair_copy(0, qx_send.at[0], qx_recv.at[0])
    load_cot.wait()
    load_wo.wait()
    qx_send[2] = mul(cot[...], wo[their_cols, :], NT).astype(bf16)
    pair_copy(2, qx_send.at[2], qx_recv.at[2])
    spread(mul(cot[...], wo[my_cols, :], NT).astype(bf16), gb, 0, True, 1.0)
    load_xf.wait()
    make_normed(xf)
    project_kv(kvf, 1)
    pair_arrived(0, qx_recv.at[0])
    spread(qx_recv[0], qb, 1, False, scale_by)
    pair_arrived(2, qx_recv.at[2])
    spread(qx_recv[2], gb, 1, True, 1.0)
    near_kv(kvb, 0, 0)
    hop_kv(kvb, 0, 0)
    send_kv(kvb, 0, 1)
    make_query(1, qf)
    pair_copy(1, qx_send.at[1], qx_recv.at[1])
    make_bias()

    def put_heads(g, i, turned, mine_ref, theirs_ref):
        place = pl.ds(pl.multiple_of(i * slab, slab), slab)
        for block, ref in enumerate((mine_ref, theirs_ref)):
            for h in range(0, SHARED, 2):
                at = (block * SHARED + h) * slab
                pair = jnp.concatenate(
                    [turned[at : at + slab, :], turned[at + slab : at + 2 * slab, :]], axis=1
                )
                to = pl.multiple_of((g * SHARED + h) * HEAD_DIM, LANES)
                ref[place, pl.ds(to, LANES)] = pair.astype(bf16)

    def folded(x):
        return x.reshape(step // FOLD, FOLD, LANES)

    def combine(tops, sums):
        top = functools.reduce(jnp.maximum, tops)
        top = jnp.max(top, axis=0, keepdims=True)
        weights = [jnp.exp(t - top) for t in tops]
        norm_sum = sum(w * s for w, s in zip(weights, sums))
        return weights, 1.0 / jnp.sum(norm_sum, axis=0, keepdims=True)

    def backward_chunk(g, chunks):
        starts = [pl.multiple_of(i * LANES, LANES) for i in chunks]
        pairs = [
            jnp.concatenate([qb[g, pl.ds(at, LANES), :], gb[g, pl.ds(at, LANES), :]], axis=0)
            for at in starts
        ]
        for u, i in enumerate(chunks):
            tops, sums, dots = [], [], []
            products = [
                mul(kvb[g, p * big : (p + 1) * big, :], pairs[u], NT) for p in range(PIECES)
            ]
            for at, part in enumerate(parts):
                within = at % SPLIT * step
                product = products[at // SPLIT][within : within + step, :]
                scores = folded(jnp.minimum(product[:, :LANES], bias[i, part, :]))
                top = jnp.max(scores, axis=0)
                expd = jnp.exp(scores - top)
                rates = folded(product[:, LANES:])
                ex[u, part, :] = expd.reshape(step, LANES)
                sd[u, part, :] = rates.reshape(step, LANES)
                tops.append(top)
                sums.append(jnp.sum(expd, axis=0))
                dots.append(jnp.sum(expd * rates, axis=0))
            weights, inverse = combine(tops, sums)
            delta = sum(w * d for w, d in zip(weights, dots))
            delta = jnp.sum(delta, axis=0, keepdims=True) * inverse
            at = u * 2 * LANES
            for part, weight in zip(parts, weights):
                probs = folded(ex[u, part, :]) * (weight * inverse)
                dscores = probs * (folded(sd[u, part, :]) - delta)
                cat[part, at + LANES : at + 2 * LANES] = probs.reshape(step, LANES).astype(bf16)
                cat[part, at : at + LANES] = dscores.reshape(step, LANES).astype(bf16)
        everything = jnp.concatenate(pairs, axis=0)
        for part in parts:
            acc[g, part, :] += mul(cat[part, :], everything)
        for u, i in enumerate(chunks):
            at = u * 2 * LANES
            turned = mul(kvt[g], cat[:, at : at + LANES])
            put_heads(g, i, turned.T * scale_by, gq_my, gq_send)

    def forward_chunk(g, chunks):
        for u, i in enumerate(chunks):
            start = pl.multiple_of(i * LANES, LANES)
            queries = qf[g, pl.ds(start, LANES), :]
            tops, sums = [], []
            products = [
                mul(kvf[g, p * big : (p + 1) * big, :], queries, NT) for p in range(PIECES)
            ]
            for at, part in enumerate(parts):
                within = at % SPLIT * step
                product = products[at // SPLIT][within : within + step, :]
                scores = folded(jnp.minimum(product, bias[i, part, :]))
                top = jnp.max(scores, axis=0)
                expd = jnp.exp(scores - top)
                ex[u, part, :] = expd.reshape(step, LANES)
                tops.append(top)
                sums.append(jnp.sum(expd, axis=0))
            weights, inverse = combine(tops, sums)
            for part, weight in zip(parts, weights):
                probs = folded(ex[u, part, :]) * (weight * inverse)
                cat[part, u * LANES : (u + 1) * LANES] = probs.reshape(step, LANES).astype(bf16)
        turned = mul(kvt[g], cat[:, : len(chunks) * LANES])
        for u, i in enumerate(chunks):
            put_heads(g, i, turned[:, u * LANES : (u + 1) * LANES].T, mix_my, mix_send)

    def run(chunk, g, begin, end, actions):
        def body(i, carry):
            for at, action in actions.items():
                pl.when(i == at)(action)
            chunk(g, [i * UNROLL + u for u in range(UNROLL)])
            return carry

        lax.fori_loop(begin, end, body, 0)

    def turn(kv_ref, g, first):
        whole = kv_ref[g].astype(f32).T
        kvt[g] = whole[first : first + HEAD_DIM, :].astype(bf16)

    def at_start():
        hop_kv(kvb, 0, 1)
        send_kv(kvf, 1, 0)

    backward_actions = [
        {0: at_start, 1: lambda: send_kv(kvf, 1, 1), 2: lambda: hop_kv(kvf, 1, 0)},
        {2: lambda: hop_sums(0)},
    ]
    for g in range(LOCAL):
        kv_arrived(kvb, 0, g, g == 0)
        turn(kvb, g, 0)
        acc[g] = jnp.zeros((total, LANES), f32)
        run(backward_chunk, g, 0, rounds, backward_actions[g])
        if g == 0:
            hop_kv(kvf, 1, 1)
        send_sums(g)
    pair_copy(3, gq_send, gq_recv)
    pair_arrived(1, qx_recv.at[1])
    spread(qx_recv[1], qf, 1, False, scale_by)

    def shift(at, src, dst, via, where, begin, end, edge, arrive_edge, turning, target):
        place = pl.ds(max(begin, mem), end - max(begin, mem))

        def copy(index, one):
            return remote(
                src.at[one], dst.at[one],
                sec_send.at[at, index], sec_recv.at[at, index], {"section": where},
            )

        small = copy(0, pl.ds(begin, mem - begin)) if begin < mem else None
        large = copy(1, place)
        around = remote(
            src.at[place], via.at[place], via_send.at[at], via_recv.at[at], {"section": edge}
        )
        onward = remote(
            via.at[place], dst.at[place],
            sec_send.at[at, 1], sec_recv.at[at, 1], {"section": target},
        )
        if detour:
            turns = jnp.logical_and(section == turning, core == 1)
            passes = jnp.logical_and(section == edge, core == 1)
        if small is not None:
            small.start()
        straight = section != edge
        if detour:
            straight = jnp.logical_and(straight, jnp.logical_not(turns))

            @pl.when(turns)
            def _():
                around.start()

        @pl.when(straight)
        def _():
            large.start()

        def pass_on():
            if detour:
                @pl.when(passes)
                def _():
                    around.wait_recv()
                    onward.start()

        def finish():
            if small is not None:
                small.wait()

            if detour:
                @pl.when(turns)
                def _():
                    around.wait_send()

                @pl.when(passes)
                def _():
                    onward.wait_send()

            @pl.when(straight)
            def _():
                large.wait_send()

            @pl.when(section != arrive_edge)
            def _():
                large.wait_recv()

        return pass_on, finish

    def attend(g, at):
        forward_chunk(g, [at * UNROLL + u for u in range(UNROLL)])
        if g == LOCAL - 1:
            place = slice(at * UNROLL * slab, (at + 1) * UNROLL * slab)
            pair_copy(4 + at, mix_send.at[place], mix_recv.at[place])

    def project_out(at):
        begin, end = at * UNROLL * slab, (at + 1) * UNROLL * slab
        place = slice(begin, end)
        made = xf[place, :].astype(f32) + mul(mix_my[place, :], wo[my_cols, :])
        pair_arrived(4 + at, mix_recv.at[place])
        made += mul(mix_recv[place, :], wo[their_cols, :])
        of[place, :] = made.astype(bf16)
        return shift(
            at, of, outf_h, via_f, after, begin, end, sections - 1, 0,
            sections // PAIR - 1, sections // PAIR,
        )

    kv_arrived(kvf, 1, 0)
    turn(kvf, 0, HEAD_DIM)
    attend(0, 0)
    attend(0, 1)
    kv_arrived(kvf, 1, 1)
    turn(kvf, 1, HEAD_DIM)
    attend(1, 0)
    hop_sums(1)
    pair_arrived(3, gq_recv)
    early[...] = mul(gq_my[...], wq[:, my_cols], NT) + mul(gq_recv[...], wq[:, their_cols], NT)
    moves = [project_out(0)]
    attend(1, 1)
    attend(0, 2)
    moves[0][0]()
    moves.append(project_out(1))

    for g in range(LOCAL):
        def arrive(count):
            place = gsend.at[g, pl.ds(0, count * rows)]
            remote(place, place, gr_send.at[g], gr_recv.at[g], {"ctx": partner}).wait_recv()

        by_place(GROUP - 1 - PAIR, GROUP - 1, arrive)
        own = acc[g, pl.ds(member * rows, rows), :]
        cross = None
        for k in range(1, GROUP):
            one = source(k)

            @pl.when(is_far(one))
            def _():
                grecv[k, g] = jnp.zeros((rows, LANES), bf16)

            value = grecv[k, g].astype(f32)
            if k % PAIR == 0:
                own = own + value
            else:
                cross = value if cross is None else cross + value
        gsum[core * LOCAL + g] = own
        gsum[other * LOCAL + g] = cross
    columns = [gsum[h, :, :HEAD_DIM] for h in range(KV_HEADS)]
    columns += [gsum[h, :, HEAD_DIM:] for h in range(KV_HEADS)]
    grad_kv = jnp.concatenate(columns, axis=1).astype(bf16)
    grad_normed = early[...] + mul(grad_kv, wkv[...], NT)
    values, scale = norm(xb[...])
    plain = values * scale
    pushed = gain_v[...].astype(f32) * grad_normed
    grad_in = cot[...].astype(f32) + scale * (
        pushed - plain * jnp.mean(pushed * plain, axis=-1, keepdims=True)
    )
    ob[...] = grad_in.astype(bf16)
    backs = [
        shift(
            rounds + p, ob, outb_h, via_b, before, p * UNROLL * slab, (p + 1) * UNROLL * slab,
            0, sections - 1, sections // PAIR, sections // PAIR - 1,
        )
        for p in range(rounds)
    ]
    attend(1, 2)
    moves[1][0]()
    moves.append(project_out(2))
    for pass_on, _ in backs:
        pass_on()
    moves[2][0]()
    moves += backs

    for copy in pair_copies:
        copy.wait_send()
    finish_kv(kvb, 0)
    finish_kv(kvf, 1)
    for g in range(LOCAL):
        finish_sums(g)
    for _, finish in moves:
        finish()


def shards(fwd_in, bwd_saved, bwd_cot, new_tokens, loss_cot, gain, w_query, w_keyval, w_out):
    section_now = lax.axis_index("section")
    sections = lax.axis_size("section")
    rows, width = fwd_in.shape[1:]
    mem = rows - new_tokens.shape[0]
    both = PAIR * rows
    total = GROUP * rows
    stack = SHARED * both
    half = width // PAIR
    rounds = stack // LANES // UNROLL
    anywhere = pl.BlockSpec(memory_space=pl.ANY)
    far_memory = pl.BlockSpec(memory_space=pltpu.HBM)
    block = jax.ShapeDtypeStruct((rows, width), bf16)
    vmem = pltpu.VMEM
    dma = pltpu.SemaphoreType.DMA
    arrived, returned = pl.pallas_call(
        functools.partial(kernel, sections, mem),
        out_shape=(block, block),
        in_specs=[far_memory] * 7,
        out_specs=(anywhere, anywhere),
        scratch_shapes=[
            vmem((rows, width), bf16), vmem((rows, width), bf16), vmem((rows, width), bf16),
            vmem((1, width), bf16),
            vmem(w_query.shape[1:], bf16), vmem(w_keyval.shape[1:], bf16), vmem(w_out.shape[1:], bf16),
            vmem((rows, width), bf16),
            vmem((LOCAL, total, LANES), bf16), vmem((LOCAL, total, LANES), bf16),
            vmem((LOCAL, HEAD_DIM, total), bf16),
            vmem((LOCAL, stack, LANES), bf16), vmem((LOCAL, stack, LANES), bf16),
            vmem((LOCAL, stack, LANES), bf16),
            vmem((rows * PAIR * SHARED // LANES, total, LANES), f32),
            vmem((UNROLL, total, LANES), f32), vmem((UNROLL, total, LANES), f32),
            vmem((total, UNROLL * 2 * LANES), bf16),
            vmem((LOCAL, total, LANES), f32), vmem((LOCAL, total, LANES), bf16),
            vmem((GROUP, LOCAL, rows, LANES), bf16), vmem((LOCAL, both, LANES), bf16),
            vmem((KV_HEADS, rows, LANES), f32), vmem((2, KV_HEADS, rows, LANES), bf16),
            vmem((3, rows, half), bf16), vmem((3, rows, half), bf16),
            vmem((rows, half), bf16), vmem((rows, half), bf16), vmem((rows, half), bf16),
            vmem((rows, half), bf16), vmem((rows, half), bf16), vmem((rows, half), bf16),
            vmem((rows, width), bf16), vmem((rows, width), bf16),
            vmem((rows, width), bf16), vmem((rows, width), bf16), vmem((rows, width), f32),
            dma((7,)), dma((4 + rounds,)), dma((4 + rounds,)),
            dma((2, LOCAL)), dma((2, LOCAL, 2)),
            dma((LOCAL,)), dma((LOCAL,)),
            dma((2 * rounds, 2)), dma((2 * rounds, 2)),
            dma((3, LOCAL)), dma((3, LOCAL)),
            dma((2 * rounds,)), dma((2 * rounds,)),
        ],
        compiler_params=pltpu.CompilerParams(
            collective_id=0, has_side_effects=True, vmem_limit_bytes=54500 * 1024
        ),
    )(
        fwd_in[0], bwd_saved[0], bwd_cot[0], pltpu.with_memory_space_constraint(gain, pltpu.HBM),
        w_query[0], w_keyval[0], w_out[0],
    )
    token_row = lax.broadcasted_iota(jnp.int32, (rows, 1), 0) >= mem
    edge = jnp.pad(new_tokens, ((mem, 0), (0, 0)))
    fwd_next = jnp.where(token_row & (section_now == 0), edge, arrived)[None]
    edge = jnp.pad(loss_cot, ((mem, 0), (0, 0)))
    cot_next = jnp.where(token_row & (section_now == sections - 1), edge, returned)[None]
    return (fwd_next, cot_next)


def solution(mesh):
    return jax.shard_map(
        shards,
        mesh=mesh,
        in_specs=(
            P("section", "ctx", None),
            P("section", "ctx", None),
            P("section", "ctx", None),
            P("ctx", None),
            P("ctx", None),
            P("section", None),
            P("section", None, None),
            P("section", None, None),
            P("section", None, None),
        ),
        out_specs=(P("section", "ctx", None), P("section", "ctx", None)),
        check_vma=False,
    )
```

```python
import functools

import jax
import jax.numpy as jnp
from jax import lax
from jax.experimental import pallas as pl
from jax.experimental.pallas import tpu as pltpu
from jax.sharding import PartitionSpec as P

HEADS = 16
KV_HEADS = 4
HEAD_DIM = 64
GROUP = 8
PAIR = 2
CHIPS = GROUP // PAIR
LOCAL = KV_HEADS // PAIR
SHARED = HEADS // KV_HEADS
LANES = 128
PIECES = 4
SPLIT = 2
FOLD = 8
UNROLL = 3

epsilon = 1e-05
far = 1 << 30
wide = 3e38

bf16 = jnp.bfloat16
f32 = jnp.float32
NT = (((1,), (1,)), ((), ()))
NN = (((1,), (0,)), ((), ()))


def mul(a, b, dims=NN):
    return lax.dot_general(a, b, dims, preferred_element_type=f32)


def kernel(
    sections, mem,
    xf_h, xb_h, cot_h, gain_h, wq_h, wkv_h, wo_h,
    outf_h, outb_h,
    xf, xb, cot, gain_v, wq, wkv, wo, normed, kvf, kvb, kvt, qf, qb, gb, bias,
    sd, ex, cat, acc, gsend, grecv, gpass, gsum, kvown, qx_send, qx_recv,
    gq_my, gq_send, gq_recv, mix_my, mix_send, mix_recv, of, ob, via_f, via_b, early,
    local_sem, pair_send, pair_recv, kv_send, kv_recv, gr_send, gr_recv, sec_send, sec_recv,
    hop_send, hop_recv, via_recv,
):
    rows = xf_h.shape[0]
    width = xf_h.shape[1]
    both = PAIR * rows
    total = GROUP * rows
    half = width // PAIR
    tokens = rows - mem
    slab = LANES // (PAIR * SHARED)
    rounds = rows // slab // UNROLL

    ctx = lax.axis_index("ctx")
    section = lax.axis_index("section")
    member = lax.rem(ctx, GROUP)
    base = ctx - member
    core = lax.rem(member, PAIR)
    chip = member // PAIR
    other = 1 - core
    partner = base + chip * PAIR + other

    after = lax.rem(section + 1, sections)
    before = lax.rem(section + sections - 1, sections)
    barrier = pltpu.get_barrier_semaphore()
    for k in range(1, GROUP):
        pl.semaphore_signal(
            barrier, inc=1, device_id={"ctx": base + lax.rem(member + k, GROUP)},
            device_id_type=pl.DeviceIdType.MESH,
        )
    detour = sections == PAIR * PAIR
    greeted = [after, before]
    if detour:
        greeted.append(lax.rem(section + PAIR, sections))
    for neighbour in greeted:
        pl.semaphore_signal(
            barrier, inc=1, device_id={"section": neighbour},
            device_id_type=pl.DeviceIdType.MESH,
        )

    loads = []
    for at, (src, dst) in enumerate(
        [
            (xb_h, xb), (gain_h, gain_v), (wkv_h, wkv), (wq_h, wq), (xf_h, xf),
            (cot_h, cot), (wo_h, wo),
        ]
    ):
        copy = pltpu.make_async_copy(src, dst, local_sem.at[at])
        copy.start()
        loads.append(copy)
    load_xb, load_gain, load_wkv, load_wq, load_xf, load_cot, load_wo = loads

    def remote(src, dst, send, recv, where):
        return pltpu.make_async_remote_copy(
            src_ref=src, dst_ref=dst, send_sem=send, recv_sem=recv,
            device_id=where, device_id_type=pl.DeviceIdType.MESH,
        )

    def pair_copy(at, src, dst):
        group = 0 if at < 3 else min(at - 2, 2)
        remote(src, dst, pair_send.at[group], pair_recv.at[at], {"ctx": partner}).start()

    def pair_arrived(at, dst):
        remote(dst, dst, pair_send.at[0], pair_recv.at[at], {"ctx": partner}).wait_recv()

    def norm(x):
        values = x.astype(f32)
        scale = lax.rsqrt(jnp.mean(values * values, axis=-1, keepdims=True) + epsilon)
        return values, scale

    def make_normed(x_ref):
        values, scale = norm(x_ref[...])
        normed[...] = (values * scale * gain_v[...].astype(f32)).astype(bf16)

    last = CHIPS - 1
    is_end = jnp.logical_or(chip == 0, chip == last)
    is_middle = jnp.logical_not(is_end)
    opposite = last - chip
    nearest_end = jnp.where(chip == 1, 0, last)
    adjacent = jnp.where(is_end, jnp.where(chip == 0, 1, last - 1), nearest_end)
    hop_at = jnp.where(chip == 0, last - 1, 1)
    hop_from = jnp.where(chip == 1, last, 0)
    hop_to = last - hop_from
    sum_via = jnp.where(chip == 0, 1, last - 1)
    sum_from = jnp.where(chip == 1, 0, last)

    def peer(k):
        return lax.rem(member + k, GROUP)

    def source(k):
        return lax.rem(member + GROUP - k, GROUP)

    def is_far(one):
        return jnp.logical_and(is_end, one // PAIR == opposite)

    order = sorted(range(1, GROUP), key=lambda k: abs(k - GROUP // 2))

    def project_kv(kv_ref, kind):
        keyval = mul(normed[...], wkv[...])
        for h in range(KV_HEADS):
            at = h * HEAD_DIM
            after_keys = KV_HEADS * HEAD_DIM + at
            kvown[kind, h] = jnp.concatenate(
                [keyval[:, at : at + HEAD_DIM], keyval[:, after_keys : after_keys + HEAD_DIM]],
                axis=1,
            ).astype(bf16)
        for g in range(LOCAL):
            kv_ref[g, pl.ds(member * rows, rows), :] = kvown[kind, core * LOCAL + g]

    def early_class(src, dst):
        ends = jnp.logical_or(dst == 0, dst == last)
        near = jnp.where(dst == 0, 1, last - 1)
        across = jnp.where(dst == 1, last, 0)
        return jnp.where(src == jnp.where(ends, near, across), 1, 0)

    def kv_copy(kv_ref, kind, g, k):
        to = peer(k)
        return remote(
            kvown.at[kind, lax.rem(to, PAIR) * LOCAL + g],
            kv_ref.at[g, pl.ds(member * rows, rows)],
            kv_send.at[kind, g], kv_recv.at[kind, g, early_class(chip, to // PAIR)],
            {"ctx": base + to},
        )

    def is_first(one):
        away = one // PAIR
        ends = jnp.logical_and(is_end, jnp.logical_or(away == hop_at, away == chip))
        return jnp.logical_or(ends, jnp.logical_and(is_middle, away == adjacent))

    def send_kv(kv_ref, kind, g, phase=None):
        for k in order:
            use = jnp.logical_not(is_far(peer(k)))
            if phase is not None:
                first = is_first(peer(k))
                use = jnp.logical_and(use, first if phase == 0 else jnp.logical_not(first))

            @pl.when(use)
            def _():
                kv_copy(kv_ref, kind, g, k).start()

    def by_place(at_end, at_middle, action):
        pl.when(is_end)(lambda: action(at_end))
        pl.when(is_middle)(lambda: action(at_middle))

    def finish_kv(kv_ref, kind):
        for g in range(LOCAL):
            def wait(count):
                place = kv_ref.at[g, pl.ds(0, count * rows)]
                remote(
                    place, place, kv_send.at[kind, g], kv_recv.at[kind, g, 0], {"ctx": partner}
                ).wait_send()

            by_place(GROUP - 1 - PAIR, GROUP - 1, wait)

            @pl.when(is_middle)
            def _():
                hop_copy(kv_ref, kind, g).wait_send()

    def hop_copy(kv_ref, kind, g):
        place = kv_ref.at[g, pl.ds(hop_from * both, both)]
        return remote(
            place, place, hop_send.at[kind, g], hop_recv.at[kind, g],
            {"ctx": base + hop_to * PAIR + core},
        )

    def kv_wait(kv_ref, kind, g, which, count):
        place = kv_ref.at[g, pl.ds(0, count * rows)]
        remote(
            place, place, kv_send.at[kind, g], kv_recv.at[kind, g, which], {"ctx": partner}
        ).wait_recv()

    def hop_kv(kv_ref, kind, g):
        @pl.when(is_middle)
        def _():
            kv_wait(kv_ref, kind, g, 1, PAIR)
            hop_copy(kv_ref, kind, g).start()

    def near_kv(kv_ref, kind, g):
        @pl.when(is_end)
        def _():
            kv_wait(kv_ref, kind, g, 1, PAIR)

    def kv_arrived(kv_ref, kind, g, near_done=False):
        by_place(
            GROUP - 1 - 2 * PAIR, GROUP - 1 - PAIR,
            lambda count: kv_wait(kv_ref, kind, g, 0, count),
        )
        if not near_done:
            near_kv(kv_ref, kind, g)

        @pl.when(is_end)
        def _():
            place = kv_ref.at[g, pl.ds(opposite * both, both)]
            remote(
                place, place, hop_send.at[kind, g], hop_recv.at[kind, g],
                {"ctx": base + opposite * PAIR + core},
            ).wait_recv()

    def gr_copy(g, k):
        to = peer(k)
        return remote(
            gsend.at[g, pl.ds(to * rows, rows)], grecv.at[k, g],
            gr_send.at[g], gr_recv.at[g], {"ctx": base + to},
        )

    def is_summed(one):
        return jnp.logical_and(is_middle, one // PAIR == last - sum_from)

    def sum_copy(g, where):
        return remote(
            gsend.at[g, pl.ds(opposite * both, both)], gpass.at[g],
            hop_send.at[2, g], hop_recv.at[2, g], {"ctx": base + where * PAIR + core},
        )

    def send_sums(g):
        gsend[g] = acc[g].astype(bf16)

        @pl.when(is_end)
        def _():
            sum_copy(g, sum_via).start()

        for k in order:
            to = peer(k)

            @pl.when(jnp.logical_not(jnp.logical_or(is_far(to), is_summed(to))))
            def _():
                gr_copy(g, k).start()

    def hop_sums(g):
        @pl.when(is_middle)
        def _():
            sum_copy(g, sum_from).wait_recv()
            place = pl.ds((last - sum_from) * both, both)
            gsend[g, place, :] = (acc[g, place, :] + gpass[g].astype(f32)).astype(bf16)
            for k in order:
                @pl.when(is_summed(peer(k)))
                def _():
                    gr_copy(g, k).start()

    def finish_sums(g):
        @pl.when(is_end)
        def _():
            sum_copy(g, sum_via).wait_send()

        def wait(count):
            place = gsend.at[g, pl.ds(0, count * rows)]
            remote(place, place, gr_send.at[g], gr_recv.at[g], {"ctx": partner}).wait_send()

        by_place(GROUP - 1 - PAIR, GROUP - 1, wait)

    def spread(matrix, dst, block, upper, factor):
        rounded = matrix.astype(f32) * factor
        zero = jnp.zeros((rows, HEAD_DIM), f32)
        for g in range(LOCAL):
            for h in range(SHARED):
                at = (g * SHARED + h) * HEAD_DIM
                piece = rounded[:, at : at + HEAD_DIM]
                parts = [zero, piece] if upper else [piece, zero]
                wide = jnp.concatenate(parts, axis=1).astype(bf16)
                for i in range(rows // slab):
                    to = i * LANES + (block * SHARED + h) * slab
                    dst[g, to : to + slab, :] = wide[i * slab : (i + 1) * slab, :]

    scale_by = HEAD_DIM ** (-0.5)
    my_cols = pl.ds(pl.multiple_of(core * half, half), half)
    their_cols = pl.ds(pl.multiple_of(other * half, half), half)

    def make_query(at, q_ref):
        qx_send[at] = mul(normed[...], wq[:, their_cols]).astype(bf16)
        spread(mul(normed[...], wq[:, my_cols]).astype(bf16), q_ref, 0, False, scale_by)

    big = total // PIECES
    step = big // SPLIT

    def make_bias():
        lane = lax.broadcasted_iota(jnp.int32, (1, LANES), 1)
        block = jnp.where(lane < LANES // PAIR, member, chip * PAIR + other)
        key = lax.broadcasted_iota(jnp.int32, (rows, LANES), 0)
        for i in range(rows // slab):
            inner = i * slab + lax.rem(lane, slab)
            position = jnp.where(inner < mem, far, block * tokens + inner - mem)
            for b in range(GROUP):
                place = jnp.where(key < mem, -1, b * tokens + key - mem)
                bias[i, b * rows : (b + 1) * rows, :] = jnp.where(place <= position, wide, -1e30)

    parts = [slice(p * step, (p + 1) * step) for p in range(PIECES * SPLIT)]

    load_xb.wait()
    load_gain.wait()
    make_normed(xb)
    load_wkv.wait()
    project_kv(kvb, 0)
    pl.semaphore_wait(barrier, GROUP - 1 + len(greeted))
    send_kv(kvb, 0, 0, 0)
    load_wq.wait()
    make_query(0, qb)
    send_kv(kvb, 0, 0, 1)
    pair_copy(0, qx_send.at[0], qx_recv.at[0])
    load_cot.wait()
    load_wo.wait()
    qx_send[2] = mul(cot[...], wo[their_cols, :], NT).astype(bf16)
    pair_copy(2, qx_send.at[2], qx_recv.at[2])
    spread(mul(cot[...], wo[my_cols, :], NT).astype(bf16), gb, 0, True, 1.0)
    load_xf.wait()
    make_normed(xf)
    project_kv(kvf, 1)
    pair_arrived(0, qx_recv.at[0])
    spread(qx_recv[0], qb, 1, False, scale_by)
    pair_arrived(2, qx_recv.at[2])
    spread(qx_recv[2], gb, 1, True, 1.0)
    near_kv(kvb, 0, 0)
    hop_kv(kvb, 0, 0)
    send_kv(kvb, 0, 1)
    make_query(1, qf)
    pair_copy(1, qx_send.at[1], qx_recv.at[1])
    make_bias()

    def put_heads(g, i, turned, mine_ref, theirs_ref):
        place = pl.ds(pl.multiple_of(i * slab, slab), slab)
        for block, ref in enumerate((mine_ref, theirs_ref)):
            for h in range(0, SHARED, 2):
                at = (block * SHARED + h) * slab
                pair = jnp.concatenate(
                    [turned[at : at + slab, :], turned[at + slab : at + 2 * slab, :]], axis=1
                )
                to = pl.multiple_of((g * SHARED + h) * HEAD_DIM, LANES)
                ref[place, pl.ds(to, LANES)] = pair.astype(bf16)

    def folded(x):
        return x.reshape(step // FOLD, FOLD, LANES)

    def combine(tops, sums):
        top = functools.reduce(jnp.maximum, tops)
        top = jnp.max(top, axis=0, keepdims=True)
        weights = [jnp.exp(t - top) for t in tops]
        norm_sum = sum(w * s for w, s in zip(weights, sums))
        return weights, 1.0 / jnp.sum(norm_sum, axis=0, keepdims=True)

    def backward_chunk(g, chunks):
        starts = [pl.multiple_of(i * LANES, LANES) for i in chunks]
        pairs = [
            jnp.concatenate([qb[g, pl.ds(at, LANES), :], gb[g, pl.ds(at, LANES), :]], axis=0)
            for at in starts
        ]
        for u, i in enumerate(chunks):
            tops, sums, dots = [], [], []
            products = [
                mul(kvb[g, p * big : (p + 1) * big, :], pairs[u], NT) for p in range(PIECES)
            ]
            for at, part in enumerate(parts):
                within = at % SPLIT * step
                product = products[at // SPLIT][within : within + step, :]
                scores = folded(jnp.minimum(product[:, :LANES], bias[i, part, :]))
                top = jnp.max(scores, axis=0)
                expd = jnp.exp(scores - top)
                rates = folded(product[:, LANES:])
                ex[u, part, :] = expd.reshape(step, LANES)
                sd[u, part, :] = rates.reshape(step, LANES)
                tops.append(top)
                sums.append(jnp.sum(expd, axis=0))
                dots.append(jnp.sum(expd * rates, axis=0))
            weights, inverse = combine(tops, sums)
            delta = sum(w * d for w, d in zip(weights, dots))
            delta = jnp.sum(delta, axis=0, keepdims=True) * inverse
            at = u * 2 * LANES
            for part, weight in zip(parts, weights):
                probs = folded(ex[u, part, :]) * (weight * inverse)
                dscores = probs * (folded(sd[u, part, :]) - delta)
                cat[part, at + LANES : at + 2 * LANES] = probs.reshape(step, LANES).astype(bf16)
                cat[part, at : at + LANES] = dscores.reshape(step, LANES).astype(bf16)
        everything = jnp.concatenate(pairs, axis=0)
        for part in parts:
            acc[g, part, :] += mul(cat[part, :], everything)
        for u, i in enumerate(chunks):
            at = u * 2 * LANES
            turned = mul(kvt[g], cat[:, at : at + LANES])
            put_heads(g, i, turned.T * scale_by, gq_my, gq_send)

    def forward_chunk(g, chunks):
        for u, i in enumerate(chunks):
            start = pl.multiple_of(i * LANES, LANES)
            queries = qf[g, pl.ds(start, LANES), :]
            tops, sums = [], []
            products = [
                mul(kvf[g, p * big : (p + 1) * big, :], queries, NT) for p in range(PIECES)
            ]
            for at, part in enumerate(parts):
                within = at % SPLIT * step
                product = products[at // SPLIT][within : within + step, :]
                scores = folded(jnp.minimum(product, bias[i, part, :]))
                top = jnp.max(scores, axis=0)
                expd = jnp.exp(scores - top)
                ex[u, part, :] = expd.reshape(step, LANES)
                tops.append(top)
                sums.append(jnp.sum(expd, axis=0))
            weights, inverse = combine(tops, sums)
            for part, weight in zip(parts, weights):
                probs = folded(ex[u, part, :]) * (weight * inverse)
                cat[part, u * LANES : (u + 1) * LANES] = probs.reshape(step, LANES).astype(bf16)
        turned = mul(kvt[g], cat[:, : len(chunks) * LANES])
        for u, i in enumerate(chunks):
            put_heads(g, i, turned[:, u * LANES : (u + 1) * LANES].T, mix_my, mix_send)

    def run(chunk, g, begin, end, actions):
        def body(i, carry):
            for at, action in actions.items():
                pl.when(i == at)(action)
            chunk(g, [i * UNROLL + u for u in range(UNROLL)])
            return carry

        lax.fori_loop(begin, end, body, 0)

    def turn(kv_ref, g, first):
        whole = kv_ref[g].astype(f32).T
        kvt[g] = whole[first : first + HEAD_DIM, :].astype(bf16)

    def at_start():
        hop_kv(kvb, 0, 1)
        send_kv(kvf, 1, 0)

    backward_actions = [
        {0: at_start, 1: lambda: send_kv(kvf, 1, 1), 2: lambda: hop_kv(kvf, 1, 0)},
        {2: lambda: hop_sums(0)},
    ]
    for g in range(LOCAL):
        kv_arrived(kvb, 0, g, g == 0)
        turn(kvb, g, 0)
        acc[g] = jnp.zeros((total, LANES), f32)
        run(backward_chunk, g, 0, rounds, backward_actions[g])
        if g == 0:
            hop_kv(kvf, 1, 1)
        send_sums(g)
    pair_copy(3, gq_send, gq_recv)
    pair_arrived(1, qx_recv.at[1])
    spread(qx_recv[1], qf, 1, False, scale_by)

    def shift(at, src, dst, via, where, begin, end, edge, arrive_edge, turning, target):
        place = pl.ds(max(begin, mem), end - max(begin, mem))

        def copy(index, one):
            return remote(
                src.at[one], dst.at[one],
                sec_send.at[at, index], sec_recv.at[at, index], {"section": where},
            )

        small = copy(0, pl.ds(begin, mem - begin)) if begin < mem else None
        large = copy(1, place)
        around = remote(
            src.at[place], via.at[place], sec_send.at[at, 1], via_recv.at[at], {"section": edge}
        )
        onward = remote(
            via.at[place], dst.at[place],
            sec_send.at[at, 1], sec_recv.at[at, 1], {"section": target},
        )
        if detour:
            turns = jnp.logical_and(section == turning, core == 1)
            passes = jnp.logical_and(section == edge, core == 1)
        if small is not None:
            small.start()
        straight = section != edge
        if detour:
            straight = jnp.logical_and(straight, jnp.logical_not(turns))

            @pl.when(turns)
            def _():
                around.start()

        @pl.when(straight)
        def _():
            large.start()

        def pass_on():
            if detour:
                @pl.when(passes)
                def _():
                    around.wait_recv()
                    onward.start()

        def finish():
            if small is not None:
                small.wait()

            if detour:
                @pl.when(turns)
                def _():
                    around.wait_send()

                @pl.when(passes)
                def _():
                    onward.wait_send()

            @pl.when(straight)
            def _():
                large.wait_send()

            @pl.when(section != arrive_edge)
            def _():
                large.wait_recv()

        return pass_on, finish

    def attend(g, at):
        forward_chunk(g, [at * UNROLL + u for u in range(UNROLL)])
        if g == LOCAL - 1:
            place = slice(at * UNROLL * slab, (at + 1) * UNROLL * slab)
            pair_copy(4 + at, mix_send.at[place], mix_recv.at[place])

    def project_out(at):
        begin, end = at * UNROLL * slab, (at + 1) * UNROLL * slab
        place = slice(begin, end)
        made = xf[place, :].astype(f32) + mul(mix_my[place, :], wo[my_cols, :])
        pair_arrived(4 + at, mix_recv.at[place])
        made += mul(mix_recv[place, :], wo[their_cols, :])
        of[place, :] = made.astype(bf16)
        return shift(
            at, of, outf_h, via_f, after, begin, end, sections - 1, 0,
            sections // PAIR - 1, sections // PAIR,
        )

    kv_arrived(kvf, 1, 0)
    turn(kvf, 0, HEAD_DIM)
    attend(0, 0)
    kv_arrived(kvf, 1, 1)
    turn(kvf, 1, HEAD_DIM)
    attend(1, 0)
    pair_arrived(3, gq_recv)
    early[...] = mul(gq_my[...], wq[:, my_cols], NT) + mul(gq_recv[...], wq[:, their_cols], NT)
    moves = [project_out(0)]
    hop_sums(1)
    attend(0, 1)
    attend(1, 1)
    moves[0][0]()
    attend(0, 2)
    moves.append(project_out(1))

    for g in range(LOCAL):
        def arrive(count):
            place = gsend.at[g, pl.ds(0, count * rows)]
            remote(place, place, gr_send.at[g], gr_recv.at[g], {"ctx": partner}).wait_recv()

        by_place(GROUP - 1 - PAIR, GROUP - 1, arrive)
        own = acc[g, pl.ds(member * rows, rows), :]
        cross = None
        for k in range(1, GROUP):
            one = source(k)

            @pl.when(is_far(one))
            def _():
                grecv[k, g] = jnp.zeros((rows, LANES), bf16)

            value = grecv[k, g].astype(f32)
            if k % PAIR == 0:
                own = own + value
            else:
                cross = value if cross is None else cross + value
        gsum[core * LOCAL + g] = own
        gsum[other * LOCAL + g] = cross
    columns = [gsum[h, :, :HEAD_DIM] for h in range(KV_HEADS)]
    columns += [gsum[h, :, HEAD_DIM:] for h in range(KV_HEADS)]
    grad_kv = jnp.concatenate(columns, axis=1).astype(bf16)
    grad_normed = early[...] + mul(grad_kv, wkv[...], NT)
    values, scale = norm(xb[...])
    plain = values * scale
    pushed = gain_v[...].astype(f32) * grad_normed
    grad_in = cot[...].astype(f32) + scale * (
        pushed - plain * jnp.mean(pushed * plain, axis=-1, keepdims=True)
    )
    ob[...] = grad_in.astype(bf16)
    backs = [
        shift(
            rounds + p, ob, outb_h, via_b, before, p * UNROLL * slab, (p + 1) * UNROLL * slab,
            0, sections - 1, sections // PAIR, sections // PAIR - 1,
        )
        for p in range(rounds)
    ]
    attend(1, 2)
    moves[1][0]()
    moves.append(project_out(2))
    for pass_on, _ in backs:
        pass_on()
    moves[2][0]()
    moves += backs

    for group, whole in enumerate((qx_send, gq_send, mix_send)):
        remote(
            whole, whole, pair_send.at[group], pair_recv.at[group], {"ctx": partner}
        ).wait_send()
    finish_kv(kvb, 0)
    finish_kv(kvf, 1)
    for g in range(LOCAL):
        finish_sums(g)
    for _, finish in moves:
        finish()


def shards(fwd_in, bwd_saved, bwd_cot, new_tokens, loss_cot, gain, w_query, w_keyval, w_out):
    section_now = lax.axis_index("section")
    sections = lax.axis_size("section")
    rows, width = fwd_in.shape[1:]
    mem = rows - new_tokens.shape[0]
    both = PAIR * rows
    total = GROUP * rows
    stack = SHARED * both
    half = width // PAIR
    rounds = stack // LANES // UNROLL
    anywhere = pl.BlockSpec(memory_space=pl.ANY)
    far_memory = pl.BlockSpec(memory_space=pltpu.HBM)
    block = jax.ShapeDtypeStruct((rows, width), bf16)
    vmem = pltpu.VMEM
    dma = pltpu.SemaphoreType.DMA
    arrived, returned = pl.pallas_call(
        functools.partial(kernel, sections, mem),
        out_shape=(block, block),
        in_specs=[far_memory] * 7,
        out_specs=(anywhere, anywhere),
        scratch_shapes=[
            vmem((rows, width), bf16), vmem((rows, width), bf16), vmem((rows, width), bf16),
            vmem((1, width), bf16),
            vmem(w_query.shape[1:], bf16), vmem(w_keyval.shape[1:], bf16), vmem(w_out.shape[1:], bf16),
            vmem((rows, width), bf16),
            vmem((LOCAL, total, LANES), bf16), vmem((LOCAL, total, LANES), bf16),
            vmem((LOCAL, HEAD_DIM, total), bf16),
            vmem((LOCAL, stack, LANES), bf16), vmem((LOCAL, stack, LANES), bf16),
            vmem((LOCAL, stack, LANES), bf16),
            vmem((rows * PAIR * SHARED // LANES, total, LANES), f32),
            vmem((UNROLL, total, LANES), f32), vmem((UNROLL, total, LANES), f32),
            vmem((total, UNROLL * 2 * LANES), bf16),
            vmem((LOCAL, total, LANES), f32), vmem((LOCAL, total, LANES), bf16),
            vmem((GROUP, LOCAL, rows, LANES), bf16), vmem((LOCAL, both, LANES), bf16),
            vmem((KV_HEADS, rows, LANES), f32), vmem((2, KV_HEADS, rows, LANES), bf16),
            vmem((3, rows, half), bf16), vmem((3, rows, half), bf16),
            vmem((rows, half), bf16), vmem((rows, half), bf16), vmem((rows, half), bf16),
            vmem((rows, half), bf16), vmem((rows, half), bf16), vmem((rows, half), bf16),
            vmem((rows, width), bf16), vmem((rows, width), bf16),
            vmem((rows, width), bf16), vmem((rows, width), bf16), vmem((rows, width), f32),
            dma((7,)), dma((3,)), dma((4 + rounds,)),
            dma((2, LOCAL)), dma((2, LOCAL, 2)),
            dma((LOCAL,)), dma((LOCAL,)),
            dma((2 * rounds, 2)), dma((2 * rounds, 2)),
            dma((3, LOCAL)), dma((3, LOCAL)),
            dma((2 * rounds,)),
        ],
        compiler_params=pltpu.CompilerParams(
            collective_id=0, has_side_effects=True, vmem_limit_bytes=54500 * 1024
        ),
    )(
        fwd_in[0], bwd_saved[0], bwd_cot[0], pltpu.with_memory_space_constraint(gain, pltpu.HBM),
        w_query[0], w_keyval[0], w_out[0],
    )
    token_row = lax.broadcasted_iota(jnp.int32, (rows, 1), 0) >= mem
    edge = jnp.pad(new_tokens, ((mem, 0), (0, 0)))
    fwd_next = jnp.where(token_row & (section_now == 0), edge, arrived)[None]
    edge = jnp.pad(loss_cot, ((mem, 0), (0, 0)))
    cot_next = jnp.where(token_row & (section_now == sections - 1), edge, returned)[None]
    return (fwd_next, cot_next)


def solution(mesh):
    return jax.shard_map(
        shards,
        mesh=mesh,
        in_specs=(
            P("section", "ctx", None),
            P("section", "ctx", None),
            P("section", "ctx", None),
            P("ctx", None),
            P("ctx", None),
            P("section", None),
            P("section", None, None),
            P("section", None, None),
            P("section", None, None),
        ),
        out_specs=(P("section", "ctx", None), P("section", "ctx", None)),
        check_vma=False,
    )
```

```python
import functools

import jax
import jax.numpy as jnp
from jax import lax
from jax.experimental import pallas as pl
from jax.experimental.pallas import tpu as pltpu
from jax.sharding import PartitionSpec as P

HEADS = 16
KV_HEADS = 4
HEAD_DIM = 64
GROUP = 8
PAIR = 2
CHIPS = GROUP // PAIR
LOCAL = KV_HEADS // PAIR
SHARED = HEADS // KV_HEADS
LANES = 128
PIECES = 2
SPLIT = 4
FOLD = 8
UNROLL = 3

epsilon = 1e-05
far = 1 << 30
wide = 3e38

bf16 = jnp.bfloat16
f32 = jnp.float32
NT = (((1,), (1,)), ((), ()))
NN = (((1,), (0,)), ((), ()))


def mul(a, b, dims=NN):
    return lax.dot_general(a, b, dims, preferred_element_type=f32)


def kernel(
    sections, mem,
    xf_h, xb_h, cot_h, gain_h, wq_h, wkv_h, wo_h,
    outf_h, outb_h,
    xf, xb, cot, gain_v, wq, wkv, wo, normed, kvf, kvb, kvt, qf, qb, gb, bias,
    sd, ex, cat, acc, gsend, grecv, gpass, gsum, kvown, qx_send, qx_recv,
    gq_my, gq_send, gq_recv, mix_my, mix_send, mix_recv, of, ob, via_f, via_b, early,
    local_sem, pair_send, pair_recv, kv_send, kv_recv, gr_send, gr_recv, sec_send, sec_recv,
    hop_send, hop_recv, via_recv,
):
    rows = xf_h.shape[0]
    width = xf_h.shape[1]
    both = PAIR * rows
    total = GROUP * rows
    half = width // PAIR
    tokens = rows - mem
    slab = LANES // (PAIR * SHARED)
    rounds = rows // slab // UNROLL

    ctx = lax.axis_index("ctx")
    section = lax.axis_index("section")
    member = lax.rem(ctx, GROUP)
    base = ctx - member
    core = lax.rem(member, PAIR)
    chip = member // PAIR
    other = 1 - core
    partner = base + chip * PAIR + other

    after = lax.rem(section + 1, sections)
    before = lax.rem(section + sections - 1, sections)
    barrier = pltpu.get_barrier_semaphore()
    for k in range(1, GROUP):
        pl.semaphore_signal(
            barrier, inc=1, device_id={"ctx": base + lax.rem(member + k, GROUP)},
            device_id_type=pl.DeviceIdType.MESH,
        )
    detour = sections == PAIR * PAIR
    greeted = [after, before]
    if detour:
        greeted.append(lax.rem(section + PAIR, sections))
    for neighbour in greeted:
        pl.semaphore_signal(
            barrier, inc=1, device_id={"section": neighbour},
            device_id_type=pl.DeviceIdType.MESH,
        )

    loads = []
    for at, (src, dst) in enumerate(
        [
            (xb_h, xb), (gain_h, gain_v), (wkv_h, wkv), (wq_h, wq), (xf_h, xf),
            (cot_h, cot), (wo_h, wo),
        ]
    ):
        copy = pltpu.make_async_copy(src, dst, local_sem.at[at])
        copy.start()
        loads.append(copy)
    load_xb, load_gain, load_wkv, load_wq, load_xf, load_cot, load_wo = loads

    def remote(src, dst, send, recv, where):
        return pltpu.make_async_remote_copy(
            src_ref=src, dst_ref=dst, send_sem=send, recv_sem=recv,
            device_id=where, device_id_type=pl.DeviceIdType.MESH,
        )

    def pair_copy(at, src, dst):
        group = 0 if at < 3 else min(at - 2, 2)
        remote(src, dst, pair_send.at[group], pair_recv.at[at], {"ctx": partner}).start()

    def pair_arrived(at, dst):
        remote(dst, dst, pair_send.at[0], pair_recv.at[at], {"ctx": partner}).wait_recv()

    def norm(x):
        values = x.astype(f32)
        scale = lax.rsqrt(jnp.mean(values * values, axis=-1, keepdims=True) + epsilon)
        return values, scale

    def make_normed(x_ref):
        values, scale = norm(x_ref[...])
        normed[...] = (values * scale * gain_v[...].astype(f32)).astype(bf16)

    last = CHIPS - 1
    is_end = jnp.logical_or(chip == 0, chip == last)
    is_middle = jnp.logical_not(is_end)
    opposite = last - chip
    nearest_end = jnp.where(chip == 1, 0, last)
    adjacent = jnp.where(is_end, jnp.where(chip == 0, 1, last - 1), nearest_end)
    hop_at = jnp.where(chip == 0, last - 1, 1)
    hop_from = jnp.where(chip == 1, last, 0)
    hop_to = last - hop_from
    sum_via = jnp.where(chip == 0, 1, last - 1)
    sum_from = jnp.where(chip == 1, 0, last)

    def peer(k):
        return lax.rem(member + k, GROUP)

    def source(k):
        return lax.rem(member + GROUP - k, GROUP)

    def is_far(one):
        return jnp.logical_and(is_end, one // PAIR == opposite)

    order = sorted(range(1, GROUP), key=lambda k: abs(k - GROUP // 2))

    def project_kv(kv_ref, kind):
        keyval = mul(normed[...], wkv[...])
        for h in range(KV_HEADS):
            at = h * HEAD_DIM
            after_keys = KV_HEADS * HEAD_DIM + at
            kvown[kind, h] = jnp.concatenate(
                [keyval[:, at : at + HEAD_DIM], keyval[:, after_keys : after_keys + HEAD_DIM]],
                axis=1,
            ).astype(bf16)
        for g in range(LOCAL):
            kv_ref[g, pl.ds(member * rows, rows), :] = kvown[kind, core * LOCAL + g]

    def early_class(src, dst):
        ends = jnp.logical_or(dst == 0, dst == last)
        near = jnp.where(dst == 0, 1, last - 1)
        across = jnp.where(dst == 1, last, 0)
        return jnp.where(src == jnp.where(ends, near, across), 1, 0)

    def kv_copy(kv_ref, kind, g, k):
        to = peer(k)
        return remote(
            kvown.at[kind, lax.rem(to, PAIR) * LOCAL + g],
            kv_ref.at[g, pl.ds(member * rows, rows)],
            kv_send.at[kind, g], kv_recv.at[kind, g, early_class(chip, to // PAIR)],
            {"ctx": base + to},
        )

    def is_first(one):
        away = one // PAIR
        ends = jnp.logical_and(is_end, jnp.logical_or(away == hop_at, away == chip))
        return jnp.logical_or(ends, jnp.logical_and(is_middle, away == adjacent))

    def send_kv(kv_ref, kind, g, phase=None):
        for k in order:
            use = jnp.logical_not(is_far(peer(k)))
            if phase is not None:
                first = is_first(peer(k))
                use = jnp.logical_and(use, first if phase == 0 else jnp.logical_not(first))

            @pl.when(use)
            def _():
                kv_copy(kv_ref, kind, g, k).start()

    def by_place(at_end, at_middle, action):
        pl.when(is_end)(lambda: action(at_end))
        pl.when(is_middle)(lambda: action(at_middle))

    def finish_kv(kv_ref, kind):
        for g in range(LOCAL):
            def wait(count):
                place = kv_ref.at[g, pl.ds(0, count * rows)]
                remote(
                    place, place, kv_send.at[kind, g], kv_recv.at[kind, g, 0], {"ctx": partner}
                ).wait_send()

            by_place(GROUP - 1 - PAIR, GROUP - 1, wait)

            @pl.when(is_middle)
            def _():
                hop_copy(kv_ref, kind, g).wait_send()

    def hop_copy(kv_ref, kind, g):
        place = kv_ref.at[g, pl.ds(hop_from * both, both)]
        return remote(
            place, place, hop_send.at[kind, g], hop_recv.at[kind, g],
            {"ctx": base + hop_to * PAIR + core},
        )

    def kv_wait(kv_ref, kind, g, which, count):
        place = kv_ref.at[g, pl.ds(0, count * rows)]
        remote(
            place, place, kv_send.at[kind, g], kv_recv.at[kind, g, which], {"ctx": partner}
        ).wait_recv()

    def hop_kv(kv_ref, kind, g):
        @pl.when(is_middle)
        def _():
            kv_wait(kv_ref, kind, g, 1, PAIR)
            hop_copy(kv_ref, kind, g).start()

    def near_kv(kv_ref, kind, g):
        @pl.when(is_end)
        def _():
            kv_wait(kv_ref, kind, g, 1, PAIR)

    def kv_arrived(kv_ref, kind, g, near_done=False):
        by_place(
            GROUP - 1 - 2 * PAIR, GROUP - 1 - PAIR,
            lambda count: kv_wait(kv_ref, kind, g, 0, count),
        )
        if not near_done:
            near_kv(kv_ref, kind, g)

        @pl.when(is_end)
        def _():
            place = kv_ref.at[g, pl.ds(opposite * both, both)]
            remote(
                place, place, hop_send.at[kind, g], hop_recv.at[kind, g],
                {"ctx": base + opposite * PAIR + core},
            ).wait_recv()

    def gr_copy(g, k):
        to = peer(k)
        return remote(
            gsend.at[g, pl.ds(to * rows, rows)], grecv.at[k, g],
            gr_send.at[g], gr_recv.at[g], {"ctx": base + to},
        )

    def is_summed(one):
        return jnp.logical_and(is_middle, one // PAIR == last - sum_from)

    def sum_copy(g, where):
        return remote(
            gsend.at[g, pl.ds(opposite * both, both)], gpass.at[g],
            hop_send.at[2, g], hop_recv.at[2, g], {"ctx": base + where * PAIR + core},
        )

    def send_sums(g):
        gsend[g] = acc[g].astype(bf16)

        @pl.when(is_end)
        def _():
            sum_copy(g, sum_via).start()

        for k in order:
            to = peer(k)

            @pl.when(jnp.logical_not(jnp.logical_or(is_far(to), is_summed(to))))
            def _():
                gr_copy(g, k).start()

    def hop_sums(g):
        @pl.when(is_middle)
        def _():
            sum_copy(g, sum_from).wait_recv()
            place = pl.ds((last - sum_from) * both, both)
            gsend[g, place, :] = (acc[g, place, :] + gpass[g].astype(f32)).astype(bf16)
            for k in order:
                @pl.when(is_summed(peer(k)))
                def _():
                    gr_copy(g, k).start()

    def finish_sums(g):
        @pl.when(is_end)
        def _():
            sum_copy(g, sum_via).wait_send()

        def wait(count):
            place = gsend.at[g, pl.ds(0, count * rows)]
            remote(place, place, gr_send.at[g], gr_recv.at[g], {"ctx": partner}).wait_send()

        by_place(GROUP - 1 - PAIR, GROUP - 1, wait)

    def spread(matrix, dst, block, upper, factor):
        rounded = matrix.astype(f32) * factor
        zero = jnp.zeros((rows, HEAD_DIM), f32)
        for g in range(LOCAL):
            for h in range(SHARED):
                at = (g * SHARED + h) * HEAD_DIM
                piece = rounded[:, at : at + HEAD_DIM]
                parts = [zero, piece] if upper else [piece, zero]
                wide = jnp.concatenate(parts, axis=1).astype(bf16)
                for i in range(rows // slab):
                    to = i * LANES + (block * SHARED + h) * slab
                    dst[g, to : to + slab, :] = wide[i * slab : (i + 1) * slab, :]

    scale_by = HEAD_DIM ** (-0.5)
    my_cols = pl.ds(pl.multiple_of(core * half, half), half)
    their_cols = pl.ds(pl.multiple_of(other * half, half), half)

    def make_query(at, q_ref):
        qx_send[at] = mul(normed[...], wq[:, their_cols]).astype(bf16)
        spread(mul(normed[...], wq[:, my_cols]).astype(bf16), q_ref, 0, False, scale_by)

    big = total // PIECES
    step = big // SPLIT

    def make_bias():
        lane = lax.broadcasted_iota(jnp.int32, (1, LANES), 1)
        block = jnp.where(lane < LANES // PAIR, member, chip * PAIR + other)
        key = lax.broadcasted_iota(jnp.int32, (rows, LANES), 0)
        for i in range(rows // slab):
            inner = i * slab + lax.rem(lane, slab)
            position = jnp.where(inner < mem, far, block * tokens + inner - mem)
            for b in range(GROUP):
                place = jnp.where(key < mem, -1, b * tokens + key - mem)
                bias[i, b * rows : (b + 1) * rows, :] = jnp.where(place <= position, wide, -1e30)

    parts = [slice(p * step, (p + 1) * step) for p in range(PIECES * SPLIT)]

    load_xb.wait()
    load_gain.wait()
    make_normed(xb)
    load_wkv.wait()
    project_kv(kvb, 0)
    pl.semaphore_wait(barrier, GROUP - 1 + len(greeted))
    send_kv(kvb, 0, 0, 0)
    load_wq.wait()
    make_query(0, qb)
    send_kv(kvb, 0, 0, 1)
    pair_copy(0, qx_send.at[0], qx_recv.at[0])
    load_cot.wait()
    load_wo.wait()
    qx_send[2] = mul(cot[...], wo[their_cols, :], NT).astype(bf16)
    pair_copy(2, qx_send.at[2], qx_recv.at[2])
    spread(mul(cot[...], wo[my_cols, :], NT).astype(bf16), gb, 0, True, 1.0)
    load_xf.wait()
    make_normed(xf)
    project_kv(kvf, 1)
    pair_arrived(0, qx_recv.at[0])
    spread(qx_recv[0], qb, 1, False, scale_by)
    pair_arrived(2, qx_recv.at[2])
    spread(qx_recv[2], gb, 1, True, 1.0)
    near_kv(kvb, 0, 0)
    hop_kv(kvb, 0, 0)
    send_kv(kvb, 0, 1)
    make_query(1, qf)
    pair_copy(1, qx_send.at[1], qx_recv.at[1])
    make_bias()

    def put_heads(g, i, turned, mine_ref, theirs_ref):
        place = pl.ds(pl.multiple_of(i * slab, slab), slab)
        for block, ref in enumerate((mine_ref, theirs_ref)):
            for h in range(0, SHARED, 2):
                at = (block * SHARED + h) * slab
                pair = jnp.concatenate(
                    [turned[at : at + slab, :], turned[at + slab : at + 2 * slab, :]], axis=1
                )
                to = pl.multiple_of((g * SHARED + h) * HEAD_DIM, LANES)
                ref[place, pl.ds(to, LANES)] = pair.astype(bf16)

    def folded(x):
        return x.reshape(step // FOLD, FOLD, LANES)

    def combine(tops, sums):
        top = functools.reduce(jnp.maximum, tops)
        top = jnp.max(top, axis=0, keepdims=True)
        weights = [jnp.exp(t - top) for t in tops]
        norm_sum = sum(w * s for w, s in zip(weights, sums))
        return weights, 1.0 / jnp.sum(norm_sum, axis=0, keepdims=True)

    def backward_chunk(g, chunks):
        starts = [pl.multiple_of(i * LANES, LANES) for i in chunks]
        pairs = [
            jnp.concatenate([qb[g, pl.ds(at, LANES), :], gb[g, pl.ds(at, LANES), :]], axis=0)
            for at in starts
        ]
        for u, i in enumerate(chunks):
            tops, sums, dots = [], [], []
            products = [
                mul(kvb[g, p * big : (p + 1) * big, :], pairs[u], NT) for p in range(PIECES)
            ]
            for at, part in enumerate(parts):
                within = at % SPLIT * step
                product = products[at // SPLIT][within : within + step, :]
                scores = folded(jnp.minimum(product[:, :LANES], bias[i, part, :]))
                top = jnp.max(scores, axis=0)
                expd = jnp.exp(scores - top)
                rates = folded(product[:, LANES:])
                ex[u, part, :] = expd.reshape(step, LANES)
                sd[u, part, :] = rates.reshape(step, LANES)
                tops.append(top)
                sums.append(jnp.sum(expd, axis=0))
                dots.append(jnp.sum(expd * rates, axis=0))
            weights, inverse = combine(tops, sums)
            delta = sum(w * d for w, d in zip(weights, dots))
            delta = jnp.sum(delta, axis=0, keepdims=True) * inverse
            at = u * 2 * LANES
            for part, weight in zip(parts, weights):
                probs = folded(ex[u, part, :]) * (weight * inverse)
                dscores = probs * (folded(sd[u, part, :]) - delta)
                cat[part, at + LANES : at + 2 * LANES] = probs.reshape(step, LANES).astype(bf16)
                cat[part, at : at + LANES] = dscores.reshape(step, LANES).astype(bf16)
        everything = jnp.concatenate(pairs, axis=0)
        for part in parts:
            acc[g, part, :] += mul(cat[part, :], everything)
        for u, i in enumerate(chunks):
            at = u * 2 * LANES
            turned = mul(kvt[g], cat[:, at : at + LANES])
            put_heads(g, i, turned.T * scale_by, gq_my, gq_send)

    def forward_chunk(g, chunks):
        for u, i in enumerate(chunks):
            start = pl.multiple_of(i * LANES, LANES)
            queries = qf[g, pl.ds(start, LANES), :]
            tops, sums = [], []
            products = [
                mul(kvf[g, p * big : (p + 1) * big, :], queries, NT) for p in range(PIECES)
            ]
            for at, part in enumerate(parts):
                within = at % SPLIT * step
                product = products[at // SPLIT][within : within + step, :]
                scores = folded(jnp.minimum(product, bias[i, part, :]))
                top = jnp.max(scores, axis=0)
                expd = jnp.exp(scores - top)
                ex[u, part, :] = expd.reshape(step, LANES)
                tops.append(top)
                sums.append(jnp.sum(expd, axis=0))
            weights, inverse = combine(tops, sums)
            for part, weight in zip(parts, weights):
                probs = folded(ex[u, part, :]) * (weight * inverse)
                cat[part, u * LANES : (u + 1) * LANES] = probs.reshape(step, LANES).astype(bf16)
        turned = mul(kvt[g], cat[:, : len(chunks) * LANES])
        for u, i in enumerate(chunks):
            put_heads(g, i, turned[:, u * LANES : (u + 1) * LANES].T, mix_my, mix_send)

    def run(chunk, g, begin, end, actions):
        def body(i, carry):
            for at, action in actions.items():
                pl.when(i == at)(action)
            chunk(g, [i * UNROLL + u for u in range(UNROLL)])
            return carry

        lax.fori_loop(begin, end, body, 0)

    def turn(kv_ref, g, first):
        whole = kv_ref[g].astype(f32).T
        kvt[g] = whole[first : first + HEAD_DIM, :].astype(bf16)

    def at_start():
        hop_kv(kvb, 0, 1)
        send_kv(kvf, 1, 0)

    backward_actions = [
        {0: at_start, 1: lambda: send_kv(kvf, 1, 1), 2: lambda: hop_kv(kvf, 1, 0)},
        {2: lambda: hop_sums(0)},
    ]
    for g in range(LOCAL):
        kv_arrived(kvb, 0, g, g == 0)
        turn(kvb, g, 0)
        acc[g] = jnp.zeros((total, LANES), f32)
        run(backward_chunk, g, 0, rounds, backward_actions[g])
        if g == 0:
            hop_kv(kvf, 1, 1)
        send_sums(g)
    pair_copy(3, gq_send, gq_recv)
    pair_arrived(1, qx_recv.at[1])
    spread(qx_recv[1], qf, 1, False, scale_by)

    def shift(at, src, dst, via, where, begin, end, edge, arrive_edge, turning, target):
        place = pl.ds(max(begin, mem), end - max(begin, mem))

        def copy(index, one):
            return remote(
                src.at[one], dst.at[one],
                sec_send.at[index], sec_recv.at[index], {"section": where},
            )

        small = copy(2 * rounds + at // rounds, pl.ds(begin, mem - begin)) if begin < mem else None
        large = copy(at, place)
        around = remote(
            src.at[place], via.at[place], sec_send.at[at], via_recv.at[at], {"section": edge}
        )
        onward = remote(
            via.at[place], dst.at[place],
            sec_send.at[at], sec_recv.at[at], {"section": target},
        )
        if detour:
            turns = jnp.logical_and(section == turning, core == 1)
            passes = jnp.logical_and(section == edge, core == 1)
        if small is not None:
            small.start()
        straight = section != edge
        if detour:
            straight = jnp.logical_and(straight, jnp.logical_not(turns))

            @pl.when(turns)
            def _():
                around.start()

        @pl.when(straight)
        def _():
            large.start()

        def pass_on():
            if detour:
                @pl.when(passes)
                def _():
                    around.wait_recv()
                    onward.start()

        def finish():
            if small is not None:
                small.wait()

            if detour:
                @pl.when(turns)
                def _():
                    around.wait_send()

                @pl.when(passes)
                def _():
                    onward.wait_send()

            @pl.when(straight)
            def _():
                large.wait_send()

            @pl.when(section != arrive_edge)
            def _():
                large.wait_recv()

        return pass_on, finish

    def attend(g, at):
        forward_chunk(g, [at * UNROLL + u for u in range(UNROLL)])
        if g == LOCAL - 1:
            place = slice(at * UNROLL * slab, (at + 1) * UNROLL * slab)
            pair_copy(4 + at, mix_send.at[place], mix_recv.at[place])

    def project_out(at):
        begin, end = at * UNROLL * slab, (at + 1) * UNROLL * slab
        place = slice(begin, end)
        made = xf[place, :].astype(f32) + mul(mix_my[place, :], wo[my_cols, :])
        pair_arrived(4 + at, mix_recv.at[place])
        made += mul(mix_recv[place, :], wo[their_cols, :])
        of[place, :] = made.astype(bf16)
        return shift(
            at, of, outf_h, via_f, after, begin, end, sections - 1, 0,
            sections // PAIR - 1, sections // PAIR,
        )

    kv_arrived(kvf, 1, 0)
    turn(kvf, 0, HEAD_DIM)
    attend(0, 0)
    kv_arrived(kvf, 1, 1)
    turn(kvf, 1, HEAD_DIM)
    attend(1, 0)
    pair_arrived(3, gq_recv)
    early[...] = mul(gq_my[...], wq[:, my_cols], NT) + mul(gq_recv[...], wq[:, their_cols], NT)
    moves = [project_out(0)]
    hop_sums(1)
    attend(0, 1)
    attend(1, 1)
    moves[0][0]()
    attend(0, 2)
    moves.append(project_out(1))

    for g in range(LOCAL):
        def arrive(count):
            place = gsend.at[g, pl.ds(0, count * rows)]
            remote(place, place, gr_send.at[g], gr_recv.at[g], {"ctx": partner}).wait_recv()

        by_place(GROUP - 1 - PAIR, GROUP - 1, arrive)
        own = acc[g, pl.ds(member * rows, rows), :]
        cross = None
        for k in range(1, GROUP):
            one = source(k)

            @pl.when(is_far(one))
            def _():
                grecv[k, g] = jnp.zeros((rows, LANES), bf16)

            value = grecv[k, g].astype(f32)
            if k % PAIR == 0:
                own = own + value
            else:
                cross = value if cross is None else cross + value
        gsum[core * LOCAL + g] = own
        gsum[other * LOCAL + g] = cross
    columns = [gsum[h, :, :HEAD_DIM] for h in range(KV_HEADS)]
    columns += [gsum[h, :, HEAD_DIM:] for h in range(KV_HEADS)]
    grad_kv = jnp.concatenate(columns, axis=1).astype(bf16)
    grad_normed = early[...] + mul(grad_kv, wkv[...], NT)
    values, scale = norm(xb[...])
    plain = values * scale
    pushed = gain_v[...].astype(f32) * grad_normed
    grad_in = cot[...].astype(f32) + scale * (
        pushed - plain * jnp.mean(pushed * plain, axis=-1, keepdims=True)
    )
    ob[...] = grad_in.astype(bf16)
    backs = [
        shift(
            rounds + p, ob, outb_h, via_b, before, p * UNROLL * slab, (p + 1) * UNROLL * slab,
            0, sections - 1, sections // PAIR, sections // PAIR - 1,
        )
        for p in range(rounds)
    ]
    attend(1, 2)
    moves[1][0]()
    moves.append(project_out(2))
    for pass_on, _ in backs:
        pass_on()
    moves[2][0]()
    moves += backs

    for group, whole in enumerate((qx_send, gq_send, mix_send)):
        remote(
            whole, whole, pair_send.at[group], pair_recv.at[group], {"ctx": partner}
        ).wait_send()
    finish_kv(kvb, 0)
    finish_kv(kvf, 1)
    for g in range(LOCAL):
        finish_sums(g)
    for _, finish in moves:
        finish()


def shards(fwd_in, bwd_saved, bwd_cot, new_tokens, loss_cot, gain, w_query, w_keyval, w_out):
    section_now = lax.axis_index("section")
    sections = lax.axis_size("section")
    rows, width = fwd_in.shape[1:]
    mem = rows - new_tokens.shape[0]
    both = PAIR * rows
    total = GROUP * rows
    stack = SHARED * both
    half = width // PAIR
    rounds = stack // LANES // UNROLL
    anywhere = pl.BlockSpec(memory_space=pl.ANY)
    far_memory = pl.BlockSpec(memory_space=pltpu.HBM)
    block = jax.ShapeDtypeStruct((rows, width), bf16)
    vmem = pltpu.VMEM
    dma = pltpu.SemaphoreType.DMA
    arrived, returned = pl.pallas_call(
        functools.partial(kernel, sections, mem),
        out_shape=(block, block),
        in_specs=[far_memory] * 7,
        out_specs=(anywhere, anywhere),
        scratch_shapes=[
            vmem((rows, width), bf16), vmem((rows, width), bf16), vmem((rows, width), bf16),
            vmem((1, width), bf16),
            vmem(w_query.shape[1:], bf16), vmem(w_keyval.shape[1:], bf16), vmem(w_out.shape[1:], bf16),
            vmem((rows, width), bf16),
            vmem((LOCAL, total, LANES), bf16), vmem((LOCAL, total, LANES), bf16),
            vmem((LOCAL, HEAD_DIM, total), bf16),
            vmem((LOCAL, stack, LANES), bf16), vmem((LOCAL, stack, LANES), bf16),
            vmem((LOCAL, stack, LANES), bf16),
            vmem((rows * PAIR * SHARED // LANES, total, LANES), f32),
            vmem((UNROLL, total, LANES), f32), vmem((UNROLL, total, LANES), f32),
            vmem((total, UNROLL * 2 * LANES), bf16),
            vmem((LOCAL, total, LANES), f32), vmem((LOCAL, total, LANES), bf16),
            vmem((GROUP, LOCAL, rows, LANES), bf16), vmem((LOCAL, both, LANES), bf16),
            vmem((KV_HEADS, rows, LANES), f32), vmem((2, KV_HEADS, rows, LANES), bf16),
            vmem((3, rows, half), bf16), vmem((3, rows, half), bf16),
            vmem((rows, half), bf16), vmem((rows, half), bf16), vmem((rows, half), bf16),
            vmem((rows, half), bf16), vmem((rows, half), bf16), vmem((rows, half), bf16),
            vmem((rows, width), bf16), vmem((rows, width), bf16),
            vmem((rows, width), bf16), vmem((rows, width), bf16), vmem((rows, width), f32),
            dma((7,)), dma((3,)), dma((4 + rounds,)),
            dma((2, LOCAL)), dma((2, LOCAL, 2)),
            dma((LOCAL,)), dma((LOCAL,)),
            dma((2 * rounds + 2,)), dma((2 * rounds + 2,)),
            dma((3, LOCAL)), dma((3, LOCAL)),
            dma((2 * rounds,)),
        ],
        compiler_params=pltpu.CompilerParams(
            collective_id=0, has_side_effects=True, vmem_limit_bytes=54500 * 1024
        ),
    )(
        fwd_in[0], bwd_saved[0], bwd_cot[0], pltpu.with_memory_space_constraint(gain, pltpu.HBM),
        w_query[0], w_keyval[0], w_out[0],
    )
    token_row = lax.broadcasted_iota(jnp.int32, (rows, 1), 0) >= mem
    edge = jnp.pad(new_tokens, ((mem, 0), (0, 0)))
    fwd_next = jnp.where(token_row & (section_now == 0), edge, arrived)[None]
    edge = jnp.pad(loss_cot, ((mem, 0), (0, 0)))
    cot_next = jnp.where(token_row & (section_now == sections - 1), edge, returned)[None]
    return (fwd_next, cot_next)


def solution(mesh):
    return jax.shard_map(
        shards,
        mesh=mesh,
        in_specs=(
            P("section", "ctx", None),
            P("section", "ctx", None),
            P("section", "ctx", None),
            P("ctx", None),
            P("ctx", None),
            P("section", None),
            P("section", None, None),
            P("section", None, None),
            P("section", None, None),
        ),
        out_specs=(P("section", "ctx", None), P("section", "ctx", None)),
        check_vma=False,
    )
```
